256 devices in a mesh: group: 2 (over x_lo), batch: 128 (over x_hi, z, y, core).
Axes of the slice: x: 4 (x_hi: 2, x_lo: 2; x = x_hi * 2 + x_lo), y: 4, z: 8, core: 2. Of those that a mesh axis runs over, the one named last changes fastest.
Arguments:
- teacher_image: bfloat16 [8192, 768], P('batch'), may hold values from -16 to 16
- teacher_text: bfloat16 [8192, 768], P('batch'), may hold values from -16 to 16
- student_image: bfloat16 [8192, 768], P('batch'), may hold values from -16 to 16
- student_text: bfloat16 [8192, 768], P('batch'), may hold values from -16 to 16
- scales: float32 [2], replicated, may hold values from 0.2 to 0.3
Outputs:
- embedding_grads: float32 [2, 8192, 768], P('group', 'batch')
The draws below stay inside these ranges and needn't reach their ends.
All inputs are finite; a program needn't handle non-finite values.
Results may differ from the reference program's by a relative error of at most 0.0031.
Values may be sent and summed in bfloat16 or wider, within the bound.
A program may use at most 64 MiB of HBM per device.

```python
import math
import jax
import jax.numpy as jnp
from jax import lax

D = 768
PAIRS = 8192


def model_draw(key, concept, share):
    keys = jax.random.split(key, 4)
    spread = float(D) ** (-0.25)
    rest = (1.0 - share * share) ** 0.5
    noise_image = jax.random.normal(keys[0], (PAIRS, D), jnp.float32)
    noise_text = jax.random.normal(keys[1], (PAIRS, D), jnp.float32)
    image_scale = jnp.exp(jax.random.uniform(keys[2], (PAIRS,), jnp.float32, jnp.log(0.6), jnp.log(6.0)))
    text_scale = jnp.exp(jax.random.uniform(keys[3], (PAIRS,), jnp.float32, jnp.log(0.6), jnp.log(6.0)))
    images = spread * image_scale[:, None] * (share * concept + rest * noise_image)
    texts = spread * text_scale[:, None] * (share * concept + rest * noise_text)
    images = jnp.clip(images, -16.0, 16.0).astype(jnp.bfloat16)
    texts = jnp.clip(texts, -16.0, 16.0).astype(jnp.bfloat16)
    return (images, texts)


def embedding_set(key):
    concept = jax.random.normal(jax.random.fold_in(key, 7101), (PAIRS, D), jnp.float32)
    teacher = model_draw(jax.random.fold_in(key, 7102), concept, 0.8)
    student = model_draw(jax.random.fold_in(key, 7103), concept, 0.6)
    return (teacher[0], teacher[1], student[0], student[1])


def draw_teacher_image(key, part):
    return embedding_set(key)[0]


def draw_teacher_text(key, part):
    return embedding_set(key)[1]


def draw_student_image(key, part):
    return embedding_set(key)[2]


def draw_student_text(key, part):
    return embedding_set(key)[3]


def setup_inputs(seed: int = 0) -> dict:
    streams_of = jax.random.split(jax.random.key(seed), 6)
    return {
        "teacher_image": draw_teacher_image(jax.random.fold_in(streams_of[5], 71), 0),
        "teacher_text": draw_teacher_text(jax.random.fold_in(streams_of[5], 71), 0),
        "student_image": draw_student_image(jax.random.fold_in(streams_of[5], 71), 0),
        "student_text": draw_student_text(jax.random.fold_in(streams_of[5], 71), 0),
        "scales": jnp.clip(jnp.exp(jax.random.uniform(streams_of[4], (2,), jnp.float32, math.log(0.2), math.log(0.3))), 0.2, 0.3),
    }


def logits(image_rows, text_rows, factor):
    return factor * lax.dot_general(image_rows, text_rows, (((1,), (1,)), ((), ())), preferred_element_type=jnp.float32)


def reference(teacher_image, teacher_text, student_image, student_text, scales):
    pair_count = teacher_image.shape[0]
    block_rows = math.gcd(pair_count, 512)
    block_count = pair_count // block_rows
    models = [(teacher_image, teacher_text, scales[0]), (student_image, student_text, scales[1])]

    def rows_at(matrix, block_index):
        return lax.dynamic_slice_in_dim(matrix, block_index * block_rows, block_rows, 0)

    def first_pass(running, block_index):
        updated = []
        row_stats = []
        for model_index in range(2):
            image_all, text_all, factor = models[model_index]
            scores_block = logits(rows_at(image_all, block_index), text_all, factor)
            row_peak = jnp.max(scores_block, axis=1)
            row_stats.append(row_peak + jnp.log(jnp.sum(jnp.exp(scores_block - row_peak[:, None]), axis=1)))
            column_peak = running[2 * model_index]
            column_total = running[2 * model_index + 1]
            peak_new = jnp.maximum(column_peak, jnp.max(scores_block, axis=0))
            column_total = column_total * jnp.exp(column_peak - peak_new) + jnp.sum(jnp.exp(scores_block - peak_new[None, :]), axis=0)
            updated.append(peak_new)
            updated.append(column_total)
        return tuple(updated), tuple(row_stats)

    lowest = jnp.full((pair_count,), -jnp.inf, jnp.float32)
    zeroes = jnp.zeros((pair_count,), jnp.float32)
    indices = jnp.arange(block_count, dtype=jnp.int32)
    column_state, row_lse = lax.scan(first_pass, (lowest, zeroes, lowest, zeroes), indices)
    row_lse = [row_lse[0].reshape(pair_count), row_lse[1].reshape(pair_count)]
    column_lse = [column_state[0] + jnp.log(column_state[1]), column_state[2] + jnp.log(column_state[3])]

    def second_pass(running, block_index):
        pieces = []
        for model_index in range(2):
            image_all, text_all, factor = models[model_index]
            scores_block = logits(rows_at(image_all, block_index), text_all, factor)
            lse_rows = lax.dynamic_slice_in_dim(row_lse[model_index], block_index * block_rows, block_rows, 0)
            row_probs = jnp.exp(scores_block - lse_rows[:, None])
            col_probs = jnp.exp(scores_block - column_lse[model_index][None, :])
            pieces.append((row_probs, col_probs))
        coupling = (0.5 * ((pieces[1][0] - pieces[0][0]) + (pieces[1][1] - pieces[0][1]))).astype(jnp.bfloat16)
        image_grad = scales[1] * jnp.dot(coupling, student_text, preferred_element_type=jnp.float32)
        running = running + jnp.dot(coupling.T, rows_at(student_image, block_index), preferred_element_type=jnp.float32)
        return running, image_grad

    text_sum, image_blocks = lax.scan(second_pass, jnp.zeros(student_image.shape, jnp.float32), indices)
    image_grad = image_blocks.reshape(student_image.shape)
    text_grad = scales[1] * text_sum
    return jnp.stack([image_grad, text_grad], axis=0)
```

```python
import jax
import jax.numpy as jnp
from jax import lax
from jax.experimental import pallas as pl
from jax.experimental.pallas import tpu as pltpu
from jax.sharding import PartitionSpec as P

MESH = pl.DeviceIdType.MESH
F32 = jnp.float32
BF16 = jnp.bfloat16
NX, NY, NZ, NC = 4, 4, 8, 2
N = 64
ROWS = NZ * N
COLS = NY * 2 * N
SENDS = 80


def device(x_hi, x_lo, y, z, core):
    return {"group": x_lo, "batch": ((x_hi * NZ + z) * NY + y) * NC + core}


def kernel(
    ti, tt, si, st, scales, out,
    rows, cols, logits, rowst, stat, rstat, cstat, rcol, cpl, cplt,
    tacc, tsend, arecv, brecv, xsend, xrecv, isend, iown, irecv, zsend, zrecv, fsend, frecv,
    lsem, ssem, rsem, csem, rssem, cssem, asem, bsem, xsem, isem, zsem, fsem,
):
    width = ti.shape[1]
    b = lax.axis_index("batch")
    g = lax.axis_index("group")
    core, y, z, xh = b % NC, (b // NC) % NY, (b // (NC * NY)) % NZ, b // (NC * NY * NZ)
    x = 2 * xh + g
    other = 1 - core
    step = 1 - 2 * core
    yu, yd, y2 = (y + 1) % NY, (y + 3) % NY, (y + 2) % NY
    source = core == g

    sibling = device(xh, g, y, z, other)
    up_y, down_y = device(xh, g, yu, z, core), device(xh, g, yd, z, core)
    across = device(1 - xh, 1 - g, y, z, core)
    beside = device(xh, 1 - g, y, z, core)
    along = device(xh, g, y, (z + step + NZ) % NZ, core)

    pending = []

    def copy(src, dst, sem, to):
        k = len(pending)
        c = pltpu.make_async_remote_copy(
            src_ref=src, dst_ref=dst, send_sem=ssem.at[k], recv_sem=sem, device_id=to, device_id_type=MESH
        )
        return c

    def send(src, dst, sem, to, when=None):
        c = copy(src, dst, sem, to)
        pending.append((c, when))
        if when is None:
            c.start()
        else:
            pl.when(when)(c.start)

    def arrived(dst, sem):
        pltpu.make_async_remote_copy(
            src_ref=dst, dst_ref=dst, send_sem=ssem.at[SENDS - 1], recv_sem=sem, device_id=sibling, device_id_type=MESH
        ).wait_recv()

    def row_at(m, k):
        return rows.at[m, pl.ds(pl.multiple_of(k * N, N), N)]

    def col_slot(yy, hi):
        return yy * 2 + hi

    def col_at(m, k):
        return cols.at[m, pl.ds(pl.multiple_of(k * N, N), N)]

    mine = col_slot(y, xh)
    locals_ = [
        pltpu.make_async_copy(tt, col_at(0, mine), lsem.at[0]),
        pltpu.make_async_copy(st, col_at(1, mine), lsem.at[1]),
    ]
    row_locals = [
        pltpu.make_async_copy(ti, row_at(0, z), lsem.at[2]),
        pltpu.make_async_copy(si, row_at(1, z), lsem.at[3]),
    ]
    for c in locals_:
        c.start()

    @pl.when(source)
    def _():
        for c in row_locals:
            c.start()

    row_me, col_me = z * NC + core, x * NY + y

    def row_peer(j):
        q = (row_me + j) % (NZ * NC)
        return q, device(xh, g, y, q // NC, q % NC)

    def col_peer(j):
        q = (col_me + j) % (NX * NY)
        qx = q // NY
        return q, device(qx // 2, qx % 2, q % NY, z, core)

    barrier = pltpu.get_barrier_semaphore()

    @pl.loop(1, 16)
    def _(j):
        pl.semaphore_signal(barrier, inc=1, device_id=row_peer(j)[1], device_id_type=MESH)
        pl.semaphore_signal(barrier, inc=1, device_id=col_peer(j)[1], device_id_type=MESH)

    pl.semaphore_wait(barrier, 30)
    for c in locals_:
        c.wait()

    @pl.when(source)
    def _():
        for c in row_locals:
            c.wait()

    m1, m2 = g, 1 - g

    def send_col(m, k, to, when=None):
        send(col_at(m, k), col_at(m, k), csem.at[m, k], to, when)

    def send_row(m, k, to, when=None):
        send(row_at(m, k), row_at(m, k), rsem.at[m, k], to, when)

    def got_col(m, k):
        arrived(col_at(m, k), csem.at[m, k])

    def got_row(m, k):
        arrived(row_at(m, k), rsem.at[m, k])

    zu, zd = (z + 1) % NZ, (z + NZ - 1) % NZ
    send_col(m1, mine, across)
    send_col(m1, mine, up_y)
    send_col(m1, mine, down_y)
    for m in (0, 1):
        send_row(m, z, device(xh, g, y, zu, 0), source)
        send_row(m, z, device(xh, g, y, zd, 1), source)
    send_col(m2, mine, up_y)
    send_col(m2, mine, down_y)
    for m in (0, 1):
        send_row(m, z, sibling, source)

    def z_hop(d, models, onward):
        k = (z - step * d + NZ) % NZ
        for m in models:
            got_row(m, k)
            if onward == "all":
                send_row(m, k, along)
            send_row(m, k, sibling)
        if onward == "own":
            send_row(core, k, along)

    def x_hop(yy):
        k = col_slot(yy, 1 - xh)
        got_col(m2, k)
        send_col(m2, k, beside)

    def y_slot(yy):
        return col_slot(yy, xh)

    z_hop(1, (0, 1), "all")
    x_hop(y)
    got_col(m1, y_slot(yd))
    send_col(m1, y_slot(yd), up_y)
    send_col(m1, y_slot(yd), across)
    got_col(m1, y_slot(yu))
    send_col(m1, y_slot(yu), across)
    z_hop(2, (0, 1), "all")
    got_col(m2, y_slot(yu))
    send_col(m2, y_slot(yu), down_y)
    got_col(m2, y_slot(yd))
    x_hop(yd)
    x_hop(yu)
    z_hop(3, (0, 1), "own")
    got_col(m1, y_slot(y2))
    send_col(m1, y_slot(y2), across)
    got_col(m2, y_slot(y2))
    z_hop(4, (core,), None)
    x_hop(y2)
    for d in (1, 2, 3):
        for m in (0, 1):
            got_row(m, (z + step * d + NZ) % NZ)
    got_row(other, (z + 4) % NZ)

    @pl.when(jnp.logical_not(source))
    def _():
        for m in (0, 1):
            got_row(m, z)

    for yy in (y, yd, yu, y2):
        got_col(m1, col_slot(yy, 1 - xh))

    for m in (0, 1):
        factor = scales[m]

        @pl.loop(0, ROWS // 256)
        def _(i):
            block = pl.ds(pl.multiple_of(i * 256, 256), 256)
            logits[m, block, :] = factor * lax.dot_general(
                rows[m, block, :], cols[m], (((1,), (1,)), ((), ())), preferred_element_type=F32
            )

    lane = lax.broadcasted_iota(jnp.int32, (N, 128), 1)
    rowst[...] = jnp.zeros_like(rowst)
    for m in (0, 1):

        def local(i, state):
            peak, total = state
            l = logits[m, pl.ds(pl.multiple_of(i * N, N), N), :]
            row_peak = jnp.max(l, axis=1, keepdims=True)
            row_lse = row_peak + jnp.log(jnp.sum(jnp.exp(l - row_peak), axis=1, keepdims=True))
            half = pl.ds(pl.multiple_of((i % 2) * N, N), N)
            rowst[half, :] = jnp.where(lane == 4 * m + i // 2, row_lse, rowst[half, :])
            now = jnp.maximum(peak, jnp.max(l, axis=0, keepdims=True))
            total = total * jnp.exp(peak - now) + jnp.sum(jnp.exp(l - now), axis=0, keepdims=True)
            return now, total

        start = (jnp.full((1, COLS), -3.0e38, F32), jnp.zeros((1, COLS), F32))
        peak, total = lax.fori_loop(0, ROWS // N, local, start)
        col_lse = peak + jnp.log(total)
        for i in range(COLS // 128):
            stat[4 * m + i : 4 * m + i + 1, :] = col_lse[:, 128 * i : 128 * (i + 1)]

    cstat[col_me] = stat[...]
    rstat[row_me] = rowst[...].T[:8, :]
    sent = len(pending)

    def stat_copy(kind, j):
        if kind == 0:
            q, to = row_peer(j)
            return pltpu.make_async_remote_copy(
                src_ref=rstat.at[row_me], dst_ref=rstat.at[row_me], send_sem=ssem.at[sent + j], recv_sem=rssem.at[row_me],
                device_id=to, device_id_type=MESH,
            ), q
        q, to = col_peer(j)
        return pltpu.make_async_remote_copy(
            src_ref=cstat.at[col_me], dst_ref=cstat.at[col_me], send_sem=cssend(j), recv_sem=cssem.at[col_me],
            device_id=to, device_id_type=MESH,
        ), q

    def cssend(j):
        return ssem.at[SENDS + j]

    @pl.loop(1, 16)
    def _(j):
        stat_copy(0, j)[0].start()
        stat_copy(1, j)[0].start()

    @pl.loop(1, 16)
    def _(j):
        q = row_peer(j)[0]
        arrived(rstat.at[q], rssem.at[q])
        q = col_peer(j)[0]
        arrived(cstat.at[q], cssem.at[q])

    @pl.loop(1, 16)
    def _(j):
        stat_copy(0, j)[0].wait_send()
        stat_copy(1, j)[0].wait_send()

    pending.extend([None] * 16)

    def joined(all_):
        peak = jnp.max(all_, axis=0)
        return peak + jnp.log(jnp.sum(jnp.exp(all_ - peak[None]), axis=0))

    stat[...] = joined(cstat[...])
    rowst[0:8, :] = joined(rstat[...])
    turned = rowst[...].T
    for m in (0, 1):
        for i in range(ROWS // 128):
            rcol[m, 128 * i : 128 * (i + 1), :] = jnp.broadcast_to(turned[:, 4 * m + i : 4 * m + i + 1], (128, 128))
    col_lse = [
        jnp.concatenate([stat[4 * m + i : 4 * m + i + 1, :] for i in range(COLS // 128)], axis=1) for m in (0, 1)
    ]

    @pl.loop(0, ROWS // 128)
    def _(i):
        block = pl.ds(pl.multiple_of(i * 128, 128), 128)
        terms = []
        for m in (0, 1):
            l = logits[m, block, :]
            r = jnp.concatenate([rcol[m, block, :]] * (COLS // 128), axis=1)
            terms.append((jnp.exp(l - r), jnp.exp(l - col_lse[m])))
        c = 0.5 * ((terms[1][0] - terms[0][0]) + (terms[1][1] - terms[0][1]))
        cpl[block, :] = c.astype(BF16)
        cplt[:, block] = c.T.astype(BF16)

    factor = scales[1]

    def text_dot(ya, yb):
        a = jnp.concatenate([cplt[pl.ds(pl.multiple_of(k * 128, 128), 128), :] for k in (ya, yb)], axis=0)
        return factor * jnp.dot(a, rows[1], preferred_element_type=F32)

    def image_dot(first):
        parts = [(z + first + k) % NZ for k in range(4)]
        a = jnp.concatenate([cpl[pl.ds(pl.multiple_of(k * N, N), N), :] for k in parts], axis=0)
        return factor * jnp.dot(a, cols[1], preferred_element_type=F32)

    far = text_dot(y2, yu)
    tacc[0:256, :] = far
    tsend[0:128, :] = far[0:128].astype(BF16)
    send(tsend.at[pl.ds(0, N)], arecv.at[0], asem.at[0], up_y)
    send(tsend.at[pl.ds(N, N)], arecv.at[1], asem.at[1], down_y)
    first = 4 * ((core + g) % 2)
    isend[...] = image_dot(4 - first).astype(BF16)
    send(isend, irecv, isem.at[0], sibling)
    tacc[256:512, :] = text_dot(yd, y)
    arrived(arecv.at[0], asem.at[0])
    tsend[128:192, :] = (tacc[128:192, :] + arecv[0].astype(F32)).astype(BF16)
    tsend[192:256, :] = tacc[192:256, :].astype(BF16)
    send(tsend.at[pl.ds(128, 128)], brecv.at[0], bsem.at[0], up_y)
    arrived(arecv.at[1], asem.at[1])
    tsend[256:320, :] = tacc[256:320, :].astype(BF16)
    tsend[320:384, :] = (tacc[320:384, :] + arecv[1].astype(F32)).astype(BF16)
    send(tsend.at[pl.ds(256, 128)], brecv.at[1], bsem.at[1], down_y)
    iown[...] = image_dot(first)
    arrived(irecv, isem.at[0])
    iown[...] = iown[...] + irecv[...].astype(F32)
    zsend[...] = iown[...].astype(BF16)
    for k in (3, 2, 1, 0):
        to = device(xh, g, y, (z + first + k) % NZ, g)
        when = None if k else jnp.logical_not(source)
        send(zsend.at[pl.ds(k * N, N)], zrecv.at[z], zsem.at[z], to, when)
    arrived(brecv.at[0], bsem.at[0])
    arrived(brecv.at[1], bsem.at[1])
    total = tacc[384:512, :] + brecv[0].astype(F32) + brecv[1].astype(F32)
    tacc[384:512, :] = total
    xsend[...] = total.astype(BF16)
    for k in (0, 1):
        send(xsend.at[pl.ds(k * N, N)], xrecv.at[x], xsem.at[x], device(k, 1, y, z, core), x != 2 * k + 1)

    @pl.when(source)
    def _():
        acc = iown[0:N, :]
        for j in range(1, NZ):
            k = (z + j) % NZ
            arrived(zrecv.at[k], zsem.at[k])
            acc = acc + zrecv[k].astype(F32)
        out[0] = acc
        fsend[...] = acc.astype(BF16)

    send(fsend, frecv, fsem.at[0], beside, jnp.logical_and(source, g == 1))

    @pl.when(jnp.logical_and(g == 0, core == 1))
    def _():
        arrived(frecv, fsem.at[0])
        out[0] = frecv[...].astype(F32)

    @pl.when(g == 1)
    def _():
        acc = tacc[pl.ds(pl.multiple_of(384 + xh * N, N), N), :]
        for j in range(1, NX):
            k = (x + j) % NX
            arrived(xrecv.at[k], xsem.at[k])
            acc = acc + xrecv[k].astype(F32)
        out[0] = acc

    for entry in pending:
        if entry is None:
            continue
        c, when = entry
        if when is None:
            c.wait_send()
        else:
            pl.when(when)(c.wait_send)


def per_device(teacher_image, teacher_text, student_image, student_text, scales):
    shard, width = teacher_image.shape
    assert shard == N
    dma = pltpu.SemaphoreType.DMA
    vmem = pltpu.VMEM
    any_ = pl.BlockSpec(memory_space=pl.ANY)
    return pl.pallas_call(
        kernel,
        out_shape=jax.ShapeDtypeStruct((1, N, width), F32),
        in_specs=[any_] * 4 + [pl.BlockSpec(memory_space=pltpu.SMEM)],
        out_specs=pl.BlockSpec(memory_space=pltpu.VMEM),
        scratch_shapes=[
            vmem((2, ROWS, width), BF16),
            vmem((2, COLS, width), BF16),
            vmem((2, ROWS, COLS), F32),
            vmem((128, 128), F32),
            vmem((8, 128), F32),
            vmem((NZ * NC, 8, 128), F32),
            vmem((NX * NY, 8, 128), F32),
            vmem((2, ROWS, 128), F32),
            vmem((ROWS, COLS), BF16),
            vmem((COLS, ROWS), BF16),
            vmem((COLS, width), F32),
            vmem((384, width), BF16),
            vmem((2, N, width), BF16),
            vmem((2, 128, width), BF16),
            vmem((128, width), BF16),
            vmem((NX, N, width), BF16),
            vmem((256, width), BF16),
            vmem((256, width), F32),
            vmem((256, width), BF16),
            vmem((256, width), BF16),
            vmem((NZ, N, width), BF16),
            vmem((N, width), BF16),
            vmem((N, width), BF16),
            dma((4,)),
            dma((SENDS + 16,)),
            dma((2, NZ)),
            dma((2, 2 * NY)),
            dma((NZ * NC,)),
            dma((NX * NY,)),
            dma((2,)),
            dma((2,)),
            dma((NX,)),
            dma((1,)),
            dma((NZ,)),
            dma((1,)),
        ],
        compiler_params=pltpu.CompilerParams(
            collective_id=0, has_side_effects=True, vmem_limit_bytes=48 * 2**20
        ),
    )(teacher_image, teacher_text, student_image, student_text, scales)


def solution(mesh):
    assert mesh.shape["group"] == 2 and mesh.shape["batch"] == 2 * NY * NZ * NC
    return jax.shard_map(
        per_device,
        mesh=mesh,
        in_specs=(P("batch", None), P("batch", None), P("batch", None), P("batch", None), P()),
        out_specs=P("group", "batch", None),
        check_vma=False,
    )
```

```python
import jax
import jax.numpy as jnp
from jax import lax
from jax.experimental import pallas as pl
from jax.experimental.pallas import tpu as pltpu
from jax.sharding import PartitionSpec as P

MESH = pl.DeviceIdType.MESH
F32 = jnp.float32
BF16 = jnp.bfloat16
NX, NY, NZ, NC = 4, 4, 8, 2
N = 64
ROWS = NZ * N
COLS = NY * 2 * N
SENDS = 80


def device(x_hi, x_lo, y, z, core):
    return {"group": x_lo, "batch": ((x_hi * NZ + z) * NY + y) * NC + core}


def kernel(
    ti, tt, si, st, scales, out,
    rows, cols, logits, rowst, stat, rstat, cstat, rcol, cpl, cplt,
    tacc, tsend, arecv, brecv, xsend, xrecv, isend, iown, irecv, zsend, zrecv, scale,
    lsem, ssem, rsem, csem, rssem, cssem, asem, bsem, xsem, isem, zsem,
):
    width = ti.shape[1]
    b = lax.axis_index("batch")
    g = lax.axis_index("group")
    core, y, z, xh = b % NC, (b // NC) % NY, (b // (NC * NY)) % NZ, b // (NC * NY * NZ)
    x = 2 * xh + g
    other = 1 - core
    step = 1 - 2 * core
    yu, yd, y2 = (y + 1) % NY, (y + 3) % NY, (y + 2) % NY
    source = core == g

    sibling = device(xh, g, y, z, other)
    up_y, down_y = device(xh, g, yu, z, core), device(xh, g, yd, z, core)
    across = device(1 - xh, 1 - g, y, z, core)
    beside = device(xh, 1 - g, y, z, core)
    along = device(xh, g, y, (z + step + NZ) % NZ, core)

    pending = []

    def copy(src, dst, sem, to):
        k = len(pending)
        c = pltpu.make_async_remote_copy(
            src_ref=src, dst_ref=dst, send_sem=ssem.at[k], recv_sem=sem, device_id=to, device_id_type=MESH
        )
        return c

    def send(src, dst, sem, to, when=None):
        c = copy(src, dst, sem, to)
        pending.append((c, when))
        if when is None:
            c.start()
        else:
            pl.when(when)(c.start)

    def finish():
        for entry in pending:
            if entry is not None:
                c, when = entry
                if when is None:
                    c.wait_send()
                else:
                    pl.when(when)(c.wait_send)

    def arrived(dst, sem):
        pltpu.make_async_remote_copy(
            src_ref=dst, dst_ref=dst, send_sem=ssem.at[SENDS - 1], recv_sem=sem, device_id=sibling, device_id_type=MESH
        ).wait_recv()

    def row_at(m, k):
        return rows.at[m, pl.ds(pl.multiple_of(k * N, N), N)]

    def col_slot(yy, hi):
        return yy * 2 + hi

    def col_at(m, k):
        return cols.at[m, pl.ds(pl.multiple_of(k * N, N), N)]

    mine = col_slot(y, xh)
    locals_ = [
        pltpu.make_async_copy(tt, col_at(0, mine), lsem.at[0]),
        pltpu.make_async_copy(st, col_at(1, mine), lsem.at[1]),
        pltpu.make_async_copy(scales, scale, lsem.at[4]),
    ]
    row_locals = [
        pltpu.make_async_copy(ti, row_at(0, z), lsem.at[2]),
        pltpu.make_async_copy(si, row_at(1, z), lsem.at[3]),
    ]
    for c in locals_:
        c.start()

    @pl.when(source)
    def _():
        for c in row_locals:
            c.start()

    row_me, col_me = z * NC + core, x * NY + y

    def row_peer(j):
        q = (row_me + j) % (NZ * NC)
        return q, device(xh, g, y, q // NC, q % NC)

    def col_peer(j):
        q = (col_me + j) % (NX * NY)
        qx = q // NY
        return q, device(qx // 2, qx % 2, q % NY, z, core)

    barrier = pltpu.get_barrier_semaphore()

    @pl.loop(1, 16)
    def _(j):
        pl.semaphore_signal(barrier, inc=1, device_id=row_peer(j)[1], device_id_type=MESH)
        pl.semaphore_signal(barrier, inc=1, device_id=col_peer(j)[1], device_id_type=MESH)

    pl.semaphore_wait(barrier, 30)
    for c in locals_:
        c.wait()

    @pl.when(source)
    def _():
        for c in row_locals:
            c.wait()

    m1, m2 = g, 1 - g

    def send_col(m, k, to, when=None):
        send(col_at(m, k), col_at(m, k), csem.at[m, k], to, when)

    def send_row(m, k, to, when=None):
        send(row_at(m, k), row_at(m, k), rsem.at[m, k], to, when)

    def got_col(m, k):
        arrived(col_at(m, k), csem.at[m, k])

    def got_row(m, k):
        arrived(row_at(m, k), rsem.at[m, k])

    zu, zd = (z + 1) % NZ, (z + NZ - 1) % NZ
    send_col(m1, mine, across)
    send_col(m1, mine, up_y)
    send_col(m1, mine, down_y)
    for m in (0, 1):
        send_row(m, z, device(xh, g, y, zu, 0), source)
        send_row(m, z, device(xh, g, y, zd, 1), source)
    send_col(m2, mine, up_y)
    send_col(m2, mine, down_y)
    for m in (0, 1):
        send_row(m, z, sibling, source)

    def z_hop(d, models, onward):
        k = (z - step * d + NZ) % NZ
        for m in models:
            got_row(m, k)
            if onward == "all":
                send_row(m, k, along)
            send_row(m, k, sibling)
        if onward == "own":
            send_row(core, k, along)

    def x_hop(yy):
        k = col_slot(yy, 1 - xh)
        got_col(m2, k)
        send_col(m2, k, beside)

    def y_slot(yy):
        return col_slot(yy, xh)

    z_hop(1, (0, 1), "all")
    x_hop(y)
    got_col(m1, y_slot(yd))
    send_col(m1, y_slot(yd), up_y)
    send_col(m1, y_slot(yd), across)
    got_col(m1, y_slot(yu))
    send_col(m1, y_slot(yu), across)
    z_hop(2, (0, 1), "all")
    got_col(m2, y_slot(yu))
    send_col(m2, y_slot(yu), down_y)
    got_col(m2, y_slot(yd))
    x_hop(yd)
    x_hop(yu)
    z_hop(3, (0, 1), "own")
    got_col(m1, y_slot(y2))
    send_col(m1, y_slot(y2), across)
    got_col(m2, y_slot(y2))
    z_hop(4, (core,), None)
    x_hop(y2)
    for d in (1, 2, 3):
        for m in (0, 1):
            got_row(m, (z + step * d + NZ) % NZ)
    got_row(other, (z + 4) % NZ)

    @pl.when(jnp.logical_not(source))
    def _():
        for m in (0, 1):
            got_row(m, z)

    for yy in (y, yd, yu, y2):
        got_col(m1, col_slot(yy, 1 - xh))

    for m in (0, 1):
        factor = scale[m]

        @pl.loop(0, ROWS // 256)
        def _(i):
            block = pl.ds(pl.multiple_of(i * 256, 256), 256)
            logits[m, block, :] = factor * lax.dot_general(
                rows[m, block, :], cols[m], (((1,), (1,)), ((), ())), preferred_element_type=F32
            )

    lane = lax.broadcasted_iota(jnp.int32, (N, 128), 1)
    rowst[...] = jnp.zeros_like(rowst)
    for m in (0, 1):

        def local(i, state):
            peak, total = state
            l = logits[m, pl.ds(pl.multiple_of(i * N, N), N), :]
            row_peak = jnp.max(l, axis=1, keepdims=True)
            row_lse = row_peak + jnp.log(jnp.sum(jnp.exp(l - row_peak), axis=1, keepdims=True))
            half = pl.ds(pl.multiple_of((i % 2) * N, N), N)
            rowst[half, :] = jnp.where(lane == 4 * m + i // 2, row_lse, rowst[half, :])
            now = jnp.maximum(peak, jnp.max(l, axis=0, keepdims=True))
            total = total * jnp.exp(peak - now) + jnp.sum(jnp.exp(l - now), axis=0, keepdims=True)
            return now, total

        start = (jnp.full((1, COLS), -3.0e38, F32), jnp.zeros((1, COLS), F32))
        peak, total = lax.fori_loop(0, ROWS // N, local, start)
        col_lse = peak + jnp.log(total)
        for i in range(COLS // 128):
            stat[4 * m + i : 4 * m + i + 1, :] = col_lse[:, 128 * i : 128 * (i + 1)]

    cstat[col_me] = stat[...]
    rstat[row_me] = rowst[...].T[:8, :]
    sent = len(pending)

    def stat_copy(kind, j):
        if kind == 0:
            q, to = row_peer(j)
            return pltpu.make_async_remote_copy(
                src_ref=rstat.at[row_me], dst_ref=rstat.at[row_me], send_sem=ssem.at[sent + j], recv_sem=rssem.at[row_me],
                device_id=to, device_id_type=MESH,
            ), q
        q, to = col_peer(j)
        return pltpu.make_async_remote_copy(
            src_ref=cstat.at[col_me], dst_ref=cstat.at[col_me], send_sem=cssend(j), recv_sem=cssem.at[col_me],
            device_id=to, device_id_type=MESH,
        ), q

    def cssend(j):
        return ssem.at[SENDS + j]

    @pl.loop(1, 16)
    def _(j):
        stat_copy(0, j)[0].start()
        stat_copy(1, j)[0].start()

    @pl.loop(1, 16)
    def _(j):
        q = row_peer(j)[0]
        arrived(rstat.at[q], rssem.at[q])
        q = col_peer(j)[0]
        arrived(cstat.at[q], cssem.at[q])

    @pl.loop(1, 16)
    def _(j):
        stat_copy(0, j)[0].wait_send()
        stat_copy(1, j)[0].wait_send()

    pending.extend([None] * 16)

    def joined(all_):
        peak = jnp.max(all_, axis=0)
        return peak + jnp.log(jnp.sum(jnp.exp(all_ - peak[None]), axis=0))

    stat[...] = joined(cstat[...])
    rowst[0:8, :] = joined(rstat[...])
    turned = rowst[...].T
    for m in (0, 1):
        for i in range(ROWS // 128):
            rcol[m, 128 * i : 128 * (i + 1), :] = jnp.broadcast_to(turned[:, 4 * m + i : 4 * m + i + 1], (128, 128))
    col_lse = [
        jnp.concatenate([stat[4 * m + i : 4 * m + i + 1, :] for i in range(COLS // 128)], axis=1) for m in (0, 1)
    ]

    @pl.loop(0, ROWS // 128)
    def _(i):
        block = pl.ds(pl.multiple_of(i * 128, 128), 128)
        terms = []
        for m in (0, 1):
            l = logits[m, block, :]
            r = jnp.concatenate([rcol[m, block, :]] * (COLS // 128), axis=1)
            terms.append((jnp.exp(l - r), jnp.exp(l - col_lse[m])))
        c = 0.5 * ((terms[1][0] - terms[0][0]) + (terms[1][1] - terms[0][1]))
        cpl[block, :] = c.astype(BF16)
        cplt[:, block] = c.T.astype(BF16)

    factor = scale[1]

    def text_dot(ya, yb):
        a = jnp.concatenate([cplt[pl.ds(pl.multiple_of(k * 128, 128), 128), :] for k in (ya, yb)], axis=0)
        return factor * jnp.dot(a, rows[1], preferred_element_type=F32)

    def image_dot(first):
        parts = [(z + first + k) % NZ for k in range(4)]
        a = jnp.concatenate([cpl[pl.ds(pl.multiple_of(k * N, N), N), :] for k in parts], axis=0)
        return factor * jnp.dot(a, cols[1], preferred_element_type=F32)

    def text_send(k, dst, sem, to):
        send(tsend.at[pl.ds(k * N, N)], dst, sem, to)

    far = text_dot(y2, yu)
    tsend[0:128, :] = far[0:128].astype(BF16)
    text_send(0, arecv.at[0], asem.at[0], up_y)
    text_send(1, arecv.at[1], asem.at[1], down_y)
    tsend[192:256, :] = far[192:256].astype(BF16)
    text_send(3, brecv.at[1], bsem.at[1], up_y)
    tacc[128:192, :] = far[128:192]
    first = 4 * ((core + g) % 2)
    isend[...] = image_dot(4 - first).astype(BF16)
    send(isend, irecv, isem.at[0], sibling)
    near = text_dot(yd, y)
    tsend[256:320, :] = near[0:64].astype(BF16)
    text_send(4, brecv.at[2], bsem.at[2], down_y)
    tacc[320:512, :] = near[64:256]
    iown[...] = image_dot(first)
    arrived(irecv, isem.at[0])
    mine_too = jnp.logical_or(g == 1, core == 1)
    for k in (3, 2, 1, 0):
        part = slice(k * N, (k + 1) * N)
        summed = iown[part, :] + irecv[part, :].astype(F32)
        if k == 0:
            iown[part, :] = summed
        zsend[part, :] = summed.astype(BF16)
        to = device(xh, 0, y, (z + first + k) % NZ, g)
        send(zsend.at[pl.ds(k * N, N)], zrecv.at[z], zsem.at[z], to, None if k else mine_too)
    arrived(arecv.at[0], asem.at[0])
    tsend[128:192, :] = (tacc[128:192, :] + arecv[0].astype(F32)).astype(BF16)
    text_send(2, brecv.at[0], bsem.at[0], up_y)
    arrived(arecv.at[1], asem.at[1])
    tsend[320:384, :] = (tacc[320:384, :] + arecv[1].astype(F32)).astype(BF16)
    text_send(5, brecv.at[3], bsem.at[3], down_y)
    for k in (1, 2, 0, 3):
        arrived(brecv.at[k], bsem.at[k])
    for k in (0, 1):
        part = slice(384 + k * N, 384 + (k + 1) * N)
        total = tacc[part, :] + (brecv[k].astype(F32) + brecv[2 + k].astype(F32))
        tacc[part, :] = total
        xsend[k * N : (k + 1) * N, :] = total.astype(BF16)
        send(xsend.at[pl.ds(k * N, N)], xrecv.at[x], xsem.at[x], device(k, 1, y, z, core), x != 2 * k + 1)

    def received(k):
        arrived(zrecv.at[k], zsem.at[k])
        return zrecv[k].astype(F32)

    @pl.when(g == 0)
    def _():
        acc = received((z + 1) % NZ)
        for j in (7, 2, 6, 3, 5, 4):
            acc = acc + received((z + j) % NZ)
        tacc[0:N, :] = acc

    @pl.when(jnp.logical_and(g == 0, core == 0))
    def _():
        out[0] = tacc[0:N, :] + iown[0:N, :]

    @pl.when(jnp.logical_and(g == 0, core == 1))
    def _():
        out[0] = tacc[0:N, :] + received(z)

    @pl.when(g == 1)
    def _():
        acc = tacc[pl.ds(pl.multiple_of(384 + xh * N, N), N), :]
        for j in range(1, NX):
            k = (x + j) % NX
            arrived(xrecv.at[k], xsem.at[k])
            acc = acc + xrecv[k].astype(F32)
        out[0] = acc

    finish()


def per_device(teacher_image, teacher_text, student_image, student_text, scales):
    shard, width = teacher_image.shape
    assert shard == N
    dma = pltpu.SemaphoreType.DMA
    vmem = pltpu.VMEM
    any_ = pl.BlockSpec(memory_space=pltpu.HBM)
    return pl.pallas_call(
        kernel,
        out_shape=jax.ShapeDtypeStruct((1, N, width), F32),
        in_specs=[any_] * 5,
        out_specs=pl.BlockSpec(memory_space=pltpu.VMEM),
        scratch_shapes=[
            vmem((2, ROWS, width), BF16),
            vmem((2, COLS, width), BF16),
            vmem((2, ROWS, COLS), F32),
            vmem((128, 128), F32),
            vmem((8, 128), F32),
            vmem((NZ * NC, 8, 128), F32),
            vmem((NX * NY, 8, 128), F32),
            vmem((2, ROWS, 128), F32),
            vmem((ROWS, COLS), BF16),
            vmem((COLS, ROWS), BF16),
            vmem((COLS, width), F32),
            vmem((384, width), BF16),
            vmem((2, N, width), BF16),
            vmem((4, N, width), BF16),
            vmem((128, width), BF16),
            vmem((NX, N, width), BF16),
            vmem((256, width), BF16),
            vmem((256, width), F32),
            vmem((256, width), BF16),
            vmem((256, width), BF16),
            vmem((NZ, N, width), BF16),
            pltpu.SMEM((2,), F32),
            dma((5,)),
            dma((SENDS + 16,)),
            dma((2, NZ)),
            dma((2, 2 * NY)),
            dma((NZ * NC,)),
            dma((NX * NY,)),
            dma((2,)),
            dma((4,)),
            dma((NX,)),
            dma((1,)),
            dma((NZ,)),
        ],
        compiler_params=pltpu.CompilerParams(
            collective_id=0, has_side_effects=True, vmem_limit_bytes=62 * 2**20
        ),
    )(teacher_image, teacher_text, student_image, student_text, scales)


def solution(mesh):
    assert mesh.shape["group"] == 2 and mesh.shape["batch"] == 2 * NY * NZ * NC
    return jax.shard_map(
        per_device,
        mesh=mesh,
        in_specs=(P("batch", None), P("batch", None), P("batch", None), P("batch", None), P()),
        out_specs=P("group", "batch", None),
        check_vma=False,
    )
```

```python
import jax
import jax.numpy as jnp
from jax import lax
from jax.experimental import pallas as pl
from jax.experimental.pallas import tpu as pltpu
from jax.sharding import PartitionSpec as P

MESH = pl.DeviceIdType.MESH
F32 = jnp.float32
BF16 = jnp.bfloat16
NX, NY, NZ, NC = 4, 4, 8, 2
N = 64
ROWS = NZ * N
COLS = NY * 2 * N
SENDS = 80


def device(x_hi, x_lo, y, z, core):
    return {"group": x_lo, "batch": ((x_hi * NZ + z) * NY + y) * NC + core}


def kernel(
    ti, tt, si, st, scales, out,
    rows, cols, logits, rowst, stat, rstat, cstat, rcol, cpl, cplt,
    tacc, tsend, arecv, brecv, xsend, xrecv, isend, iown, irecv, zsend, zrecv, scale,
    lsem, ssem, stsem, rsem, csem, rssem, cssem, asem, bsem, xsem, isem, zsem,
):
    width = ti.shape[1]
    b = lax.axis_index("batch")
    g = lax.axis_index("group")
    core, y, z, xh = b % NC, (b // NC) % NY, (b // (NC * NY)) % NZ, b // (NC * NY * NZ)
    x = 2 * xh + g
    other = 1 - core
    step = 1 - 2 * core
    yu, yd, y2 = (y + 1) % NY, (y + 3) % NY, (y + 2) % NY
    source = core == g

    sibling = device(xh, g, y, z, other)
    up_y, down_y = device(xh, g, yu, z, core), device(xh, g, yd, z, core)
    across = device(1 - xh, 1 - g, y, z, core)
    beside = device(xh, 1 - g, y, z, core)
    along = device(xh, g, y, (z + step + NZ) % NZ, core)

    pending = []

    def copy(src, dst, sem, to):
        k = len(pending)
        c = pltpu.make_async_remote_copy(
            src_ref=src, dst_ref=dst, send_sem=ssem.at[k], recv_sem=sem, device_id=to, device_id_type=MESH
        )
        return c

    def send(src, dst, sem, to, when=None):
        c = copy(src, dst, sem, to)
        pending.append((c, when))
        if when is None:
            c.start()
        else:
            pl.when(when)(c.start)

    def finish():
        assert len(pending) < SENDS
        for entry in pending:
            if entry is not None:
                c, when = entry
                if when is None:
                    c.wait_send()
                else:
                    pl.when(when)(c.wait_send)

    def arrived(dst, sem):
        pltpu.make_async_remote_copy(
            src_ref=dst, dst_ref=dst, send_sem=ssem.at[SENDS - 1], recv_sem=sem, device_id=sibling, device_id_type=MESH
        ).wait_recv()

    def row_at(m, k):
        return rows.at[m, pl.ds(pl.multiple_of(k * N, N), N)]

    def col_slot(yy, hi):
        return yy * 2 + hi

    def col_at(m, k):
        return cols.at[m, pl.ds(pl.multiple_of(k * N, N), N)]

    mine = col_slot(y, xh)
    locals_ = [
        pltpu.make_async_copy(tt, col_at(0, mine), lsem.at[0]),
        pltpu.make_async_copy(st, col_at(1, mine), lsem.at[1]),
        pltpu.make_async_copy(scales, scale, lsem.at[4]),
    ]
    row_locals = [
        pltpu.make_async_copy(ti, row_at(0, z), lsem.at[2]),
        pltpu.make_async_copy(si, row_at(1, z), lsem.at[3]),
    ]
    for c in locals_:
        c.start()

    @pl.when(source)
    def _():
        for c in row_locals:
            c.start()

    row_me, col_me = z * NC + core, x * NY + y

    def row_peer(j):
        q = (row_me + j) % (NZ * NC)
        return q, device(xh, g, y, q // NC, q % NC)

    def col_peer(j):
        q = (col_me + j) % (NX * NY)
        qx = q // NY
        return q, device(qx // 2, qx % 2, q % NY, z, core)

    barrier = pltpu.get_barrier_semaphore()

    @pl.loop(1, 16)
    def _(j):
        pl.semaphore_signal(barrier, inc=1, device_id=row_peer(j)[1], device_id_type=MESH)
        pl.semaphore_signal(barrier, inc=1, device_id=col_peer(j)[1], device_id_type=MESH)

    pl.semaphore_wait(barrier, 30)
    for c in locals_:
        c.wait()

    @pl.when(source)
    def _():
        for c in row_locals:
            c.wait()

    def send_col(m, k, to):
        send(col_at(m, k), col_at(m, k), csem.at[m, k], to)

    def send_row(m, k, to, when=None):
        send(row_at(m, k), row_at(m, k), rsem.at[m, k], to, when)

    def got_col(m, k):
        arrived(col_at(m, k), csem.at[m, k])

    def got_row(m, k):
        arrived(row_at(m, k), rsem.at[m, k])

    def z_from(d):
        return (z - step * d + NZ) % NZ

    def z_start(m, d):
        send_row(m, z, device(xh, g, y, (z + d) % NZ, 0), source)
        send_row(m, z, device(xh, g, y, (z + NZ - d) % NZ, 1), source)

    def z_pass(m):
        k = z_from(2)
        got_row(m, k)
        send_row(m, k, device(xh, g, y, (z + step + NZ) % NZ, core))
        send_row(m, k, device(xh, g, y, (z + 2 * step + NZ) % NZ, core), core == m)
        send_row(m, k, sibling)

    def y_start(m):
        send_col(m, mine, device(xh, g, y2, z, core))
        send_col(m, mine, up_y)
        send_col(m, mine, down_y)

    def x_pass(m):
        k = col_slot(y, 1 - xh)
        got_col(m, k)
        send_col(m, k, up_y)
        send_col(m, k, down_y)

    def y_pass(m):
        k = col_slot(y2, xh)
        got_col(m, k)
        send_col(m, k, across)

    def z_rest(m):
        for d in (1, 3):
            got_row(m, z_from(d))
            send_row(m, z_from(d), sibling)
        far = z_from(4)

        @pl.when(core == m)
        def _():
            got_row(m, far)

        send_row(m, far, sibling, core == m)

    def complete(m):
        for yy in (yu, yd):
            got_col(m, col_slot(yy, xh))
            got_col(m, col_slot(yy, 1 - xh))
        got_col(m, col_slot(y2, 1 - xh))
        for d in (1, 2, 3):
            got_row(m, (z + step * d + NZ) % NZ)

        @pl.when(core != m)
        def _():
            got_row(m, (z + 4) % NZ)

        @pl.when(jnp.logical_not(source))
        def _():
            got_row(m, z)

    send_col(0, mine, across)
    z_start(0, 2)
    y_start(0)
    z_start(0, 1)
    send_col(1, mine, across)
    z_start(1, 2)
    send_row(0, z, sibling, source)
    x_pass(0)
    y_start(1)
    z_pass(0)
    z_start(1, 1)
    send_row(1, z, sibling, source)
    y_pass(0)
    x_pass(1)
    z_pass(1)
    y_pass(1)
    z_rest(0)
    complete(0)

    lane = lax.broadcasted_iota(jnp.int32, (N, 128), 1)

    def tile(m):
        factor = scale[m]

        @pl.loop(0, ROWS // 256)
        def _(i):
            block = pl.ds(pl.multiple_of(i * 256, 256), 256)
            logits[m, block, :] = factor * lax.dot_general(
                rows[m, block, :], cols[m], (((1,), (1,)), ((), ())), preferred_element_type=F32
            )

    def local_stats(m):
        rowst[...] = jnp.zeros_like(rowst)

        def local(i, state):
            peak, total = state
            l = logits[m, pl.ds(pl.multiple_of(i * N, N), N), :]
            row_peak = jnp.max(l, axis=1, keepdims=True)
            row_lse = row_peak + jnp.log(jnp.sum(jnp.exp(l - row_peak), axis=1, keepdims=True))
            half = pl.ds(pl.multiple_of((i % 2) * N, N), N)
            rowst[half, :] = jnp.where(lane == i // 2, row_lse, rowst[half, :])
            now = jnp.maximum(peak, jnp.max(l, axis=0, keepdims=True))
            total = total * jnp.exp(peak - now) + jnp.sum(jnp.exp(l - now), axis=0, keepdims=True)
            return now, total

        start = (jnp.full((1, COLS), -3.0e38, F32), jnp.zeros((1, COLS), F32))
        peak, total = lax.fori_loop(0, ROWS // N, local, start)
        col_lse = peak + jnp.log(total)
        parts = [col_lse[:, 128 * i : 128 * (i + 1)] for i in range(COLS // 128)]
        cstat[m, col_me] = jnp.concatenate(parts + [jnp.zeros((8 - len(parts), 128), F32)], axis=0)
        rstat[m, row_me] = rowst[...].T[:8, :]

    def stat_copies(m, j):
        return [
            pltpu.make_async_remote_copy(
                src_ref=ref.at[m, me], dst_ref=ref.at[m, me], send_sem=stsem.at[m, kind, j], recv_sem=sem.at[m, me],
                device_id=peer(j)[1], device_id_type=MESH,
            )
            for kind, (ref, sem, me, peer) in enumerate(
                ((rstat, rssem, row_me, row_peer), (cstat, cssem, col_me, col_peer))
            )
        ]

    def stats_start(m):
        @pl.loop(1, 16)
        def _(j):
            for c in stat_copies(m, j):
                c.start()

    def joined(all_):
        peak = jnp.max(all_, axis=0)
        return peak + jnp.log(jnp.sum(jnp.exp(all_ - peak[None]), axis=0))

    def stats_end(m):
        @pl.loop(1, 16)
        def _(j):
            arrived(rstat.at[m, row_peer(j)[0]], rssem.at[m, row_peer(j)[0]])
            arrived(cstat.at[m, col_peer(j)[0]], cssem.at[m, col_peer(j)[0]])

        stat[...] = joined(cstat[m])
        rowst[0:8, :] = joined(rstat[m])
        turned = rowst[...].T
        for i in range(ROWS // 128):
            rcol[m, 128 * i : 128 * (i + 1), :] = jnp.broadcast_to(turned[:, i : i + 1], (128, 128))
        return jnp.concatenate([stat[i : i + 1, :] for i in range(COLS // 128)], axis=1)

    def chances(m, block, col_lse):
        l = logits[m, block, :]
        r = jnp.concatenate([rcol[m, block, :]] * (COLS // 128), axis=1)
        return jnp.exp(l - r) + jnp.exp(l - col_lse)

    tile(0)
    local_stats(0)
    stats_start(0)
    z_rest(1)
    complete(1)
    tile(1)
    local_stats(1)
    stats_start(1)
    teacher_lse = stats_end(0)

    @pl.loop(0, ROWS // 128)
    def _(i):
        block = pl.ds(pl.multiple_of(i * 128, 128), 128)
        logits[0, block, :] = chances(0, block, teacher_lse)

    student_lse = stats_end(1)

    @pl.loop(0, ROWS // 128)
    def _(i):
        block = pl.ds(pl.multiple_of(i * 128, 128), 128)
        c = 0.5 * (chances(1, block, student_lse) - logits[0, block, :])
        cpl[block, :] = c.astype(BF16)
        cplt[:, block] = c.T.astype(BF16)

    for m in (0, 1):

        @pl.loop(1, 16)
        def _(j):
            for c in stat_copies(m, j):
                c.wait_send()

    factor = scale[1]

    def text_dot(ya, yb):
        a = jnp.concatenate([cplt[pl.ds(pl.multiple_of(k * 128, 128), 128), :] for k in (ya, yb)], axis=0)
        return factor * jnp.dot(a, rows[1], preferred_element_type=F32)

    def image_dot(first):
        parts = [(z + first + k) % NZ for k in range(4)]
        a = jnp.concatenate([cpl[pl.ds(pl.multiple_of(k * N, N), N), :] for k in parts], axis=0)
        return factor * jnp.dot(a, cols[1], preferred_element_type=F32)

    def text_send(k, dst, sem, to):
        send(tsend.at[pl.ds(k * N, N)], dst, sem, to)

    far = text_dot(y2, yu)
    tsend[0:128, :] = far[0:128].astype(BF16)
    text_send(0, arecv.at[0], asem.at[0], up_y)
    text_send(1, arecv.at[1], asem.at[1], down_y)
    tsend[192:256, :] = far[192:256].astype(BF16)
    text_send(3, brecv.at[1], bsem.at[1], up_y)
    tacc[128:192, :] = far[128:192]
    first = 4 * ((core + g) % 2)
    isend[...] = image_dot(4 - first).astype(BF16)
    send(isend, irecv, isem.at[0], sibling)
    near = text_dot(yd, y)
    tsend[256:320, :] = near[0:64].astype(BF16)
    text_send(4, brecv.at[2], bsem.at[2], down_y)
    tacc[320:512, :] = near[64:256]
    iown[...] = image_dot(first)
    arrived(irecv, isem.at[0])
    mine_too = jnp.logical_or(g == 1, core == 1)
    for k in (3, 2, 1, 0):
        part = slice(k * N, (k + 1) * N)
        summed = iown[part, :] + irecv[part, :].astype(F32)
        if k == 0:
            iown[part, :] = summed
        zsend[part, :] = summed.astype(BF16)
        to = device(xh, 0, y, (z + first + k) % NZ, g)
        send(zsend.at[pl.ds(k * N, N)], zrecv.at[z], zsem.at[z], to, None if k else mine_too)
    arrived(arecv.at[0], asem.at[0])
    tsend[128:192, :] = (tacc[128:192, :] + arecv[0].astype(F32)).astype(BF16)
    text_send(2, brecv.at[0], bsem.at[0], up_y)
    arrived(arecv.at[1], asem.at[1])
    tsend[320:384, :] = (tacc[320:384, :] + arecv[1].astype(F32)).astype(BF16)
    text_send(5, brecv.at[3], bsem.at[3], down_y)
    for k in (1, 2, 0, 3):
        arrived(brecv.at[k], bsem.at[k])
    for k in (0, 1):
        part = slice(384 + k * N, 384 + (k + 1) * N)
        total = tacc[part, :] + (brecv[k].astype(F32) + brecv[2 + k].astype(F32))
        tacc[part, :] = total
        xsend[k * N : (k + 1) * N, :] = total.astype(BF16)
        send(xsend.at[pl.ds(k * N, N)], xrecv.at[x], xsem.at[x], device(k, 1, y, z, core), x != 2 * k + 1)

    def received(k):
        arrived(zrecv.at[k], zsem.at[k])
        return zrecv[k].astype(F32)

    @pl.when(g == 0)
    def _():
        acc = received((z + 1) % NZ)
        for j in (7, 2, 6, 3, 5, 4):
            acc = acc + received((z + j) % NZ)
        tacc[0:N, :] = acc

    @pl.when(jnp.logical_and(g == 0, core == 0))
    def _():
        out[0] = tacc[0:N, :] + iown[0:N, :]

    @pl.when(jnp.logical_and(g == 0, core == 1))
    def _():
        out[0] = tacc[0:N, :] + received(z)

    @pl.when(g == 1)
    def _():
        acc = tacc[pl.ds(pl.multiple_of(384 + xh * N, N), N), :]
        for j in range(1, NX):
            k = (x + j) % NX
            arrived(xrecv.at[k], xsem.at[k])
            acc = acc + xrecv[k].astype(F32)
        out[0] = acc

    finish()


def per_device(teacher_image, teacher_text, student_image, student_text, scales):
    shard, width = teacher_image.shape
    assert shard == N
    dma = pltpu.SemaphoreType.DMA
    vmem = pltpu.VMEM
    any_ = pl.BlockSpec(memory_space=pltpu.HBM)
    return pl.pallas_call(
        kernel,
        out_shape=jax.ShapeDtypeStruct((1, N, width), F32),
        in_specs=[any_] * 5,
        out_specs=pl.BlockSpec(memory_space=pltpu.VMEM),
        scratch_shapes=[
            vmem((2, ROWS, width), BF16),
            vmem((2, COLS, width), BF16),
            vmem((2, ROWS, COLS), F32),
            vmem((128, 128), F32),
            vmem((8, 128), F32),
            vmem((2, NZ * NC, 8, 128), F32),
            vmem((2, NX * NY, 8, 128), F32),
            vmem((2, ROWS, 128), F32),
            vmem((ROWS, COLS), BF16),
            vmem((COLS, ROWS), BF16),
            vmem((COLS, width), F32),
            vmem((384, width), BF16),
            vmem((2, N, width), BF16),
            vmem((4, N, width), BF16),
            vmem((128, width), BF16),
            vmem((NX, N, width), BF16),
            vmem((256, width), BF16),
            vmem((256, width), F32),
            vmem((256, width), BF16),
            vmem((256, width), BF16),
            vmem((NZ, N, width), BF16),
            pltpu.SMEM((2,), F32),
            dma((5,)),
            dma((SENDS,)),
            dma((2, 2, 16)),
            dma((2, NZ)),
            dma((2, 2 * NY)),
            dma((2, NZ * NC)),
            dma((2, NX * NY)),
            dma((2,)),
            dma((4,)),
            dma((NX,)),
            dma((1,)),
            dma((NZ,)),
        ],
        compiler_params=pltpu.CompilerParams(
            collective_id=0, has_side_effects=True, vmem_limit_bytes=62 * 2**20
        ),
    )(teacher_image, teacher_text, student_image, student_text, scales)


def solution(mesh):
    assert mesh.shape["group"] == 2 and mesh.shape["batch"] == 2 * NY * NZ * NC
    return jax.shard_map(
        per_device,
        mesh=mesh,
        in_specs=(P("batch", None), P("batch", None), P("batch", None), P("batch", None), P()),
        out_specs=P("group", "batch", None),
        check_vma=False,
    )
```

```python
import functools

import jax
import jax.numpy as jnp
from jax import lax
from jax.experimental import pallas as pl
from jax.experimental.pallas import tpu as pltpu
from jax.sharding import PartitionSpec as P

MESH = pl.DeviceIdType.MESH
F32 = jnp.float32
BF16 = jnp.bfloat16
NX, NY, NZ, NC = 4, 4, 8, 2
N = 64
ROWS = NZ * N
COLS = NY * 2 * N
SENDS = 80
FAR_FIRST = (8, 9, 7, 6, 10, 5, 11, 4, 12, 3, 13, 2, 14, 1, 15)


def mod(a, n):
    return lax.rem(a, jnp.int32(n))


def div(a, n):
    return lax.div(a, jnp.int32(n))


def device(x_hi, x_lo, y, z, core):
    return {"group": x_lo, "batch": ((x_hi * NZ + z) * NY + y) * NC + core}


def kernel(
    ti, tt, si, st, scales, out,
    rows, cols, logits, stat, rstat, cstat, rcol, cpl, cplt,
    tacc, tsend, arecv, brecv, xsend, xrecv, isend, iown, irecv, zsend, zrecv, scale,
    lsem, ssem, stsem, rsem, csem, rssem, cssem, asem, bsem, xsem, isem, zsem,
):
    width = ti.shape[1]
    b = lax.axis_index("batch")
    g = lax.axis_index("group")
    core, y, z, xh = mod(b, NC), mod(div(b, NC), NY), mod(div(b, NC * NY), NZ), div(b, NC * NY * NZ)
    x = 2 * xh + g
    other = 1 - core
    step = 1 - 2 * core
    yu, yd, y2 = mod(y + 1, NY), mod(y + 3, NY), mod(y + 2, NY)
    source = core == g

    sibling = device(xh, g, y, z, other)
    up_y, down_y = device(xh, g, yu, z, core), device(xh, g, yd, z, core)
    across = device(1 - xh, 1 - g, y, z, core)
    beside = device(xh, 1 - g, y, z, core)

    pending = []

    def copy(src, dst, sem, to):
        k = len(pending)
        c = pltpu.make_async_remote_copy(
            src_ref=src, dst_ref=dst, send_sem=ssem.at[k], recv_sem=sem, device_id=to, device_id_type=MESH
        )
        return c

    def send(src, dst, sem, to, when=None):
        c = copy(src, dst, sem, to)
        pending.append((c, when))
        if when is None:
            c.start()
        else:
            pl.when(when)(c.start)

    def finish():
        assert len(pending) < SENDS
        for entry in pending:
            if entry is not None:
                c, when = entry
                if when is None:
                    c.wait_send()
                else:
                    pl.when(when)(c.wait_send)

    def arrived(dst, sem):
        pltpu.make_async_remote_copy(
            src_ref=dst, dst_ref=dst, send_sem=ssem.at[SENDS - 1], recv_sem=sem, device_id=sibling, device_id_type=MESH
        ).wait_recv()

    def row_at(m, k):
        return rows.at[m, pl.ds(pl.multiple_of(k * N, N), N)]

    def col_slot(yy, hi):
        return yy * 2 + hi

    def col_at(m, k):
        return cols.at[m, pl.ds(pl.multiple_of(k * N, N), N)]

    row_me, col_me = z * NC + core, x * NY + y

    def row_peer(j):
        q = mod(row_me + j, NZ * NC)
        return q, device(xh, g, y, div(q, NC), mod(q, NC))

    def col_peer(j):
        q = mod(col_me + j, NX * NY)
        qx = div(q, NY)
        return q, device(div(qx, 2), mod(qx, 2), mod(q, NY), z, core)

    barrier = pltpu.get_barrier_semaphore()

    @pl.loop(1, 16)
    def _(j):
        pl.semaphore_signal(barrier, inc=1, device_id=row_peer(j)[1], device_id_type=MESH)
        pl.semaphore_signal(barrier, inc=1, device_id=col_peer(j)[1], device_id_type=MESH)

    mine = col_slot(y, xh)
    locals_ = [
        pltpu.make_async_copy(tt, col_at(0, mine), lsem.at[0]),
        pltpu.make_async_copy(st, col_at(1, mine), lsem.at[1]),
        pltpu.make_async_copy(scales, scale, lsem.at[4]),
    ]
    row_locals = [
        pltpu.make_async_copy(ti, row_at(0, z), lsem.at[2]),
        pltpu.make_async_copy(si, row_at(1, z), lsem.at[3]),
    ]
    for c in locals_:
        c.start()

    @pl.when(source)
    def _():
        for c in row_locals:
            c.start()

    pl.semaphore_wait(barrier, 30)
    def send_col(m, k, to):
        src = (tt, st)[m] if k is mine else col_at(m, k)
        send(src, col_at(m, k), csem.at[m, k], to)

    def send_row(m, k, to, when=None):
        src = (ti, si)[m] if k is z else row_at(m, k)
        send(src, row_at(m, k), rsem.at[m, k], to, when)

    def got_col(m, k):
        arrived(col_at(m, k), csem.at[m, k])

    def got_row(m, k):
        arrived(row_at(m, k), rsem.at[m, k])

    def z_from(d):
        return mod(z - step * d + NZ, NZ)

    def z_start(m, d):
        send_row(m, z, device(xh, g, y, mod(z + d, NZ), 0), source)
        send_row(m, z, device(xh, g, y, mod(z + NZ - d, NZ), 1), source)

    def z_own(m):
        z_start(m, 2)
        z_start(m, 1)
        send_row(m, z, sibling, source)

    def z_pass(m):
        k = z_from(2)
        got_row(m, k)
        send_row(m, k, device(xh, g, y, mod(z + 2 * step + NZ, NZ), core), core == m)
        send_row(m, k, device(xh, g, y, mod(z + step + NZ, NZ), core))
        send_row(m, k, sibling)

    def y_start(m):
        send_col(m, mine, device(xh, g, y2, z, core))
        send_col(m, mine, up_y)
        send_col(m, mine, down_y)

    def x_pass(m):
        k = col_slot(y, 1 - xh)
        got_col(m, k)
        send_col(m, k, up_y)
        send_col(m, k, down_y)

    def y_pass(m):
        k = col_slot(y2, xh)
        got_col(m, k)
        send_col(m, k, across)

    def z_rest(m):
        got_row(m, z_from(1))
        send_row(m, z_from(1), sibling)
        far = z_from(4)

        @pl.when(core == m)
        def _():
            got_row(m, far)

        send_row(m, far, sibling, core == m)
        got_row(m, z_from(3))
        send_row(m, z_from(3), sibling)

    def complete(m):
        for yy in (yu, yd):
            got_col(m, col_slot(yy, xh))
            got_col(m, col_slot(yy, 1 - xh))
        got_col(m, col_slot(y2, 1 - xh))
        for d in (1, 2, 3):
            got_row(m, mod(z + step * d + NZ, NZ))

        @pl.when(core != m)
        def _():
            got_row(m, mod(z + 4, NZ))

        @pl.when(jnp.logical_not(source))
        def _():
            got_row(m, z)

    send_col(0, mine, across)
    z_start(0, 2)
    y_start(0)
    z_start(0, 1)
    send_row(0, z, sibling, source)
    z_start(1, 2)
    send_col(1, mine, across)
    y_start(1)
    z_start(1, 1)
    send_row(1, z, sibling, source)
    x_pass(0)
    z_pass(0)
    y_pass(0)
    x_pass(1)
    z_pass(1)
    y_pass(1)
    z_rest(0)
    complete(0)
    for c in locals_:
        c.wait()

    @pl.when(source)
    def _():
        for c in row_locals:
            c.wait()

    def tile(m):
        factor = scale[m]

        @pl.loop(0, ROWS // 256)
        def _(i):
            block = pl.ds(pl.multiple_of(i * 256, 256), 256)
            logits[m, block, :] = factor * lax.dot_general(
                rows[m, block, :], cols[m], (((1,), (1,)), ((), ())), preferred_element_type=F32
            )

    def local_stats(m):
        peak, total = jnp.full((8, COLS), -3.0e38, F32), jnp.zeros((8, COLS), F32)
        row_lse = []
        for i in range(ROWS // 128):
            l = logits[m, 128 * i : 128 * (i + 1), :]
            parts = [l[:, 128 * k : 128 * (k + 1)] for k in range(COLS // 128)]
            lane_peak = functools.reduce(jnp.maximum, parts)
            lane_total = functools.reduce(jnp.add, [jnp.exp(p - lane_peak) for p in parts])
            lane_peak, lane_total = lane_peak.T, lane_total.T
            row_peak = jnp.max(lane_peak, axis=0, keepdims=True)
            row_total = jnp.sum(lane_total * jnp.exp(lane_peak - row_peak), axis=0, keepdims=True)
            row_lse.append(row_peak + jnp.log(row_total))
            l = l.reshape(16, 8, COLS)
            now = jnp.maximum(peak, jnp.max(l, axis=0))
            total = total * jnp.exp(peak - now) + jnp.sum(jnp.exp(l - now[None]), axis=0)
            peak = now
        col_peak = jnp.max(peak, axis=0, keepdims=True)
        col_lse = col_peak + jnp.log(jnp.sum(total * jnp.exp(peak - col_peak), axis=0, keepdims=True))
        parts = [col_lse[:, 128 * i : 128 * (i + 1)] for i in range(COLS // 128)]
        rest = [jnp.zeros((4, 128), F32)]
        cstat[m, col_me] = jnp.concatenate(parts + rest, axis=0)
        rstat[m, row_me] = jnp.concatenate(row_lse + rest, axis=0)

    def stat_copies(m, j):
        return [
            pltpu.make_async_remote_copy(
                src_ref=ref.at[m, me], dst_ref=ref.at[m, me], send_sem=stsem.at[m, kind, j], recv_sem=sem.at[m, me],
                device_id=peer(j)[1], device_id_type=MESH,
            )
            for kind, (ref, sem, me, peer) in enumerate(
                ((rstat, rssem, row_me, row_peer), (cstat, cssem, col_me, col_peer))
            )
        ]

    def stats_start(m):
        for j in FAR_FIRST:
            for c in stat_copies(m, j):
                c.start()

    def joined(all_):
        peak = jnp.max(all_, axis=0)
        return peak + jnp.log(jnp.sum(jnp.exp(all_ - peak[None]), axis=0))

    def stats_end(m):
        @pl.loop(1, 16)
        def _(j):
            arrived(rstat.at[m, row_peer(j)[0]], rssem.at[m, row_peer(j)[0]])
            arrived(cstat.at[m, col_peer(j)[0]], cssem.at[m, col_peer(j)[0]])

        stat[...] = joined(cstat[m])
        turned = jnp.concatenate([joined(rstat[m]), jnp.zeros((120, 128), F32)], axis=0).T
        for i in range(ROWS // 128):
            rcol[m, 128 * i : 128 * (i + 1), :] = jnp.broadcast_to(turned[:, i : i + 1], (128, 128))
        return jnp.concatenate([stat[i : i + 1, :] for i in range(COLS // 128)], axis=1)

    def chances(m, block, col_lse):
        l = logits[m, block, :]
        r = jnp.concatenate([rcol[m, block, :]] * (COLS // 128), axis=1)
        return jnp.exp(l - r) + jnp.exp(l - col_lse)

    tile(0)
    z_rest(1)
    local_stats(0)
    stats_start(0)
    complete(1)
    tile(1)
    local_stats(1)
    stats_start(1)
    teacher_lse = stats_end(0)

    @pl.loop(0, ROWS // 128)
    def _(i):
        block = pl.ds(pl.multiple_of(i * 128, 128), 128)
        logits[0, block, :] = chances(0, block, teacher_lse)

    student_lse = stats_end(1)

    @pl.loop(0, ROWS // 128)
    def _(i):
        block = pl.ds(pl.multiple_of(i * 128, 128), 128)
        c = 0.5 * (chances(1, block, student_lse) - logits[0, block, :])
        cpl[block, :] = c.astype(BF16)
        cplt[:, block] = c.T.astype(BF16)

    for m in (0, 1):

        @pl.loop(1, 16)
        def _(j):
            for c in stat_copies(m, j):
                c.wait_send()

    factor = scale[1]

    def text_dot(ya, yb):
        a = jnp.concatenate([cplt[pl.ds(pl.multiple_of(k * 128, 128), 128), :] for k in (ya, yb)], axis=0)
        return factor * jnp.dot(a, rows[1], preferred_element_type=F32)

    def image_dot(first):
        parts = [mod(z + first + k, NZ) for k in range(4)]
        a = jnp.concatenate([cpl[pl.ds(pl.multiple_of(k * N, N), N), :] for k in parts], axis=0)
        return factor * jnp.dot(a, cols[1], preferred_element_type=F32)

    def text_send(k, dst, sem, to):
        send(tsend.at[pl.ds(k * N, N)], dst, sem, to)

    far = text_dot(y2, yu)
    tsend[0:128, :] = far[0:128].astype(BF16)
    text_send(0, arecv.at[0], asem.at[0], up_y)
    text_send(1, arecv.at[1], asem.at[1], down_y)
    tsend[192:256, :] = far[192:256].astype(BF16)
    text_send(3, brecv.at[1], bsem.at[1], up_y)
    tacc[128:192, :] = far[128:192]
    first = 4 * mod(core + g, 2)
    isend[...] = image_dot(4 - first).astype(BF16)
    send(isend, irecv, isem.at[0], sibling)
    near = text_dot(yd, y)
    tsend[256:320, :] = near[0:64].astype(BF16)
    text_send(4, brecv.at[2], bsem.at[2], down_y)
    tacc[320:512, :] = near[64:256]
    iown[...] = image_dot(first)
    arrived(irecv, isem.at[0])
    mine_too = jnp.logical_or(g == 1, core == 1)
    for k in (3, 2, 1, 0):
        part = slice(k * N, (k + 1) * N)
        summed = iown[part, :] + irecv[part, :].astype(F32)
        if k == 0:
            iown[part, :] = summed
        zsend[part, :] = summed.astype(BF16)
        to = device(xh, 0, y, mod(z + first + k, NZ), g)
        send(zsend.at[pl.ds(k * N, N)], zrecv.at[z], zsem.at[z], to, None if k else mine_too)
    arrived(arecv.at[0], asem.at[0])
    tsend[128:192, :] = (tacc[128:192, :] + arecv[0].astype(F32)).astype(BF16)
    text_send(2, brecv.at[0], bsem.at[0], up_y)
    arrived(arecv.at[1], asem.at[1])
    tsend[320:384, :] = (tacc[320:384, :] + arecv[1].astype(F32)).astype(BF16)
    text_send(5, brecv.at[3], bsem.at[3], down_y)
    for k in (1, 2, 0, 3):
        arrived(brecv.at[k], bsem.at[k])
    for k in (0, 1):
        part = slice(384 + k * N, 384 + (k + 1) * N)
        total = tacc[part, :] + (brecv[k].astype(F32) + brecv[2 + k].astype(F32))
        tacc[part, :] = total
        xsend[k * N : (k + 1) * N, :] = total.astype(BF16)
        send(xsend.at[pl.ds(k * N, N)], xrecv.at[x], xsem.at[x], device(k, 1, y, z, core), x != 2 * k + 1)

    def received(k):
        arrived(zrecv.at[k], zsem.at[k])
        return zrecv[k].astype(F32)

    @pl.when(g == 0)
    def _():
        acc = received(mod(z + 1, NZ))
        for j in (7, 2, 6, 3, 5, 4):
            acc = acc + received(mod(z + j, NZ))
        tacc[0:N, :] = acc

    @pl.when(jnp.logical_and(g == 0, core == 0))
    def _():
        out[0] = tacc[0:N, :] + iown[0:N, :]

    @pl.when(jnp.logical_and(g == 0, core == 1))
    def _():
        out[0] = tacc[0:N, :] + received(z)

    @pl.when(g == 1)
    def _():
        acc = tacc[pl.ds(pl.multiple_of(384 + xh * N, N), N), :]
        for j in range(1, NX):
            k = mod(x + j, NX)
            arrived(xrecv.at[k], xsem.at[k])
            acc = acc + xrecv[k].astype(F32)
        out[0] = acc

    finish()


def per_device(teacher_image, teacher_text, student_image, student_text, scales):
    shard, width = teacher_image.shape
    assert shard == N
    dma = pltpu.SemaphoreType.DMA
    vmem = pltpu.VMEM
    any_ = pl.BlockSpec(memory_space=pltpu.HBM)
    return pl.pallas_call(
        kernel,
        out_shape=jax.ShapeDtypeStruct((1, N, width), F32),
        in_specs=[any_] * 5,
        out_specs=pl.BlockSpec(memory_space=pltpu.VMEM),
        scratch_shapes=[
            vmem((2, ROWS, width), BF16),
            vmem((2, COLS, width), BF16),
            vmem((2, ROWS, COLS), F32),
            vmem((8, 128), F32),
            vmem((2, NZ * NC, 8, 128), F32),
            vmem((2, NX * NY, 8, 128), F32),
            vmem((2, ROWS, 128), F32),
            vmem((ROWS, COLS), BF16),
            vmem((COLS, ROWS), BF16),
            vmem((COLS, width), F32),
            vmem((384, width), BF16),
            vmem((2, N, width), BF16),
            vmem((4, N, width), BF16),
            vmem((128, width), BF16),
            vmem((NX, N, width), BF16),
            vmem((256, width), BF16),
            vmem((256, width), F32),
            vmem((256, width), BF16),
            vmem((256, width), BF16),
            vmem((NZ, N, width), BF16),
            pltpu.SMEM((2,), F32),
            dma((5,)),
            dma((SENDS,)),
            dma((2, 2, 16)),
            dma((2, NZ)),
            dma((2, 2 * NY)),
            dma((2, NZ * NC)),
            dma((2, NX * NY)),
            dma((2,)),
            dma((4,)),
            dma((NX,)),
            dma((1,)),
            dma((NZ,)),
        ],
        compiler_params=pltpu.CompilerParams(
            collective_id=0, has_side_effects=True, vmem_limit_bytes=62 * 2**20
        ),
    )(teacher_image, teacher_text, student_image, student_text, scales)


def solution(mesh):
    assert mesh.shape["group"] == 2 and mesh.shape["batch"] == 2 * NY * NZ * NC
    return jax.shard_map(
        per_device,
        mesh=mesh,
        in_specs=(P("batch", None), P("batch", None), P("batch", None), P("batch", None), P()),
        out_specs=P("group", "batch", None),
        check_vma=False,
    )
```

```python
import functools

import jax
import jax.numpy as jnp
from jax import lax
from jax.experimental import pallas as pl
from jax.experimental.pallas import tpu as pltpu
from jax.sharding import PartitionSpec as P

MESH = pl.DeviceIdType.MESH
F32 = jnp.float32
BF16 = jnp.bfloat16
NX, NY, NZ, NC = 4, 4, 8, 2
N = 64
ROWS = NZ * N
COLS = NY * 2 * N
SENDS = 80
FAR_FIRST = (8, 9, 7, 6, 10, 5, 11, 4, 12, 3, 13, 2, 14, 1, 15)


def mod(a, n):
    return lax.rem(a, jnp.int32(n))


def div(a, n):
    return lax.div(a, jnp.int32(n))


def device(x_hi, x_lo, y, z, core):
    return {"group": x_lo, "batch": ((x_hi * NZ + z) * NY + y) * NC + core}


def kernel(
    ti, tt, si, st, scales, out,
    rows, cols, logits, stat, rstat, cstat, rcol, cpl, cplt,
    tacc, tsend, arecv, brecv, xsend, xrecv, isend, iown, irecv, zsend, zrecv, crecv, scale,
    lsem, ssem, stsem, rsem, csem, rssem, cssem, asem, bsem, xsem, isem, zsem, tosem,
):
    width = ti.shape[1]
    b = lax.axis_index("batch")
    g = lax.axis_index("group")
    core, y, z, xh = mod(b, NC), mod(div(b, NC), NY), mod(div(b, NC * NY), NZ), div(b, NC * NY * NZ)
    x = 2 * xh + g
    other = 1 - core
    step = 1 - 2 * core
    yu, yd, y2 = mod(y + 1, NY), mod(y + 3, NY), mod(y + 2, NY)
    source = core == g

    sibling = device(xh, g, y, z, other)
    up_y, down_y = device(xh, g, yu, z, core), device(xh, g, yd, z, core)
    across = device(1 - xh, 1 - g, y, z, core)
    beside = device(xh, 1 - g, y, z, core)

    pending = []

    def copy(src, dst, sem, to):
        k = len(pending)
        c = pltpu.make_async_remote_copy(
            src_ref=src, dst_ref=dst, send_sem=ssem.at[k], recv_sem=sem, device_id=to, device_id_type=MESH
        )
        return c

    def send(src, dst, sem, to, when=None):
        c = copy(src, dst, sem, to)
        pending.append((c, when))
        if when is None:
            c.start()
        else:
            pl.when(when)(c.start)

    def finish():
        assert len(pending) < SENDS
        for entry in pending:
            if entry is not None:
                c, when = entry
                if when is None:
                    c.wait_send()
                else:
                    pl.when(when)(c.wait_send)

    def arrived(dst, sem):
        pltpu.make_async_remote_copy(
            src_ref=dst, dst_ref=dst, send_sem=ssem.at[SENDS - 1], recv_sem=sem, device_id=sibling, device_id_type=MESH
        ).wait_recv()

    def row_at(m, k):
        return rows.at[m, pl.ds(pl.multiple_of(k * N, N), N)]

    def col_slot(yy, hi):
        return yy * 2 + hi

    def col_at(m, k):
        return cols.at[m, pl.ds(pl.multiple_of(k * N, N), N)]

    row_me, col_me = z * NC + core, x * NY + y

    def row_peer(j):
        q = mod(row_me + j, NZ * NC)
        return q, device(xh, g, y, div(q, NC), mod(q, NC))

    def col_peer(j):
        q = mod(col_me + j, NX * NY)
        qx = div(q, NY)
        return q, device(div(qx, 2), mod(qx, 2), mod(q, NY), z, core)

    barrier = pltpu.get_barrier_semaphore()

    near = [sibling, up_y, down_y, device(xh, g, y2, z, core), across, beside]
    near += [device(xh, g, y, mod(z + d, NZ), c) for d in (1, 7, 2, 6) for c in (0, 1)]
    for to in near:
        pl.semaphore_signal(barrier, inc=1, device_id=to, device_id_type=MESH)

    mine = col_slot(y, xh)
    locals_ = [
        pltpu.make_async_copy(tt, col_at(0, mine), lsem.at[0]),
        pltpu.make_async_copy(st, col_at(1, mine), lsem.at[1]),
        pltpu.make_async_copy(scales, scale, lsem.at[4]),
    ]
    row_locals = [
        pltpu.make_async_copy(ti, row_at(0, z), lsem.at[2]),
        pltpu.make_async_copy(si, row_at(1, z), lsem.at[3]),
    ]
    for c in locals_:
        c.start()

    @pl.when(source)
    def _():
        for c in row_locals:
            c.start()

    pl.semaphore_wait(barrier, len(near))
    def send_col(m, k, to):
        src = (tt, st)[m] if k is mine else col_at(m, k)
        send(src, col_at(m, k), csem.at[m, k], to)

    def send_row(m, k, to, when=None):
        src = (ti, si)[m] if k is z else row_at(m, k)
        send(src, row_at(m, k), rsem.at[m, k], to, when)

    def got_col(m, k):
        arrived(col_at(m, k), csem.at[m, k])

    def got_row(m, k):
        arrived(row_at(m, k), rsem.at[m, k])

    def z_from(d):
        return mod(z - step * d + NZ, NZ)

    def z_start(m, d):
        send_row(m, z, device(xh, g, y, mod(z + d, NZ), 0), source)
        send_row(m, z, device(xh, g, y, mod(z + NZ - d, NZ), 1), source)

    def z_own(m):
        z_start(m, 2)
        z_start(m, 1)
        send_row(m, z, sibling, source)

    def z_pass(m):
        k = z_from(2)
        got_row(m, k)
        send_row(m, k, device(xh, g, y, mod(z + 2 * step + NZ, NZ), core), core == m)
        send_row(m, k, device(xh, g, y, mod(z + step + NZ, NZ), core))
        send_row(m, k, sibling)

    def y_start(m):
        send_col(m, mine, device(xh, g, y2, z, core))
        send_col(m, mine, up_y)
        send_col(m, mine, down_y)

    def x_pass(m):
        k = col_slot(y, 1 - xh)
        got_col(m, k)
        send_col(m, k, up_y)
        send_col(m, k, down_y)

    def y_pass(m):
        k = col_slot(y2, xh)
        got_col(m, k)
        send_col(m, k, across)

    def z_rest(m):
        got_row(m, z_from(1))
        send_row(m, z_from(1), sibling)
        far = z_from(4)

        @pl.when(core == m)
        def _():
            got_row(m, far)

        send_row(m, far, sibling, core == m)
        got_row(m, z_from(3))
        send_row(m, z_from(3), sibling)

    def complete(m):
        for yy in (yu, yd):
            got_col(m, col_slot(yy, xh))
            got_col(m, col_slot(yy, 1 - xh))
        got_col(m, col_slot(y2, 1 - xh))
        for d in (1, 2, 3):
            got_row(m, mod(z + step * d + NZ, NZ))

        @pl.when(core != m)
        def _():
            got_row(m, mod(z + 4, NZ))

        @pl.when(jnp.logical_not(source))
        def _():
            got_row(m, z)

    send_col(0, mine, across)
    z_start(0, 2)
    y_start(0)
    z_start(0, 1)
    send_row(0, z, sibling, source)
    z_start(1, 2)
    send_col(1, mine, across)
    y_start(1)
    z_start(1, 1)
    send_row(1, z, sibling, source)
    x_pass(0)
    z_pass(0)
    y_pass(0)
    x_pass(1)
    z_pass(1)
    y_pass(1)
    z_rest(0)
    complete(0)
    for c in locals_:
        c.wait()

    @pl.when(source)
    def _():
        for c in row_locals:
            c.wait()

    def tile(m):
        factor = scale[m]

        @pl.loop(0, ROWS // 256)
        def _(i):
            block = pl.ds(pl.multiple_of(i * 256, 256), 256)
            logits[m, block, :] = factor * lax.dot_general(
                rows[m, block, :], cols[m], (((1,), (1,)), ((), ())), preferred_element_type=F32
            )

    def local_stats(m):
        peak, total = jnp.full((8, COLS), -3.0e38, F32), jnp.zeros((8, COLS), F32)
        row_lse = []
        for i in range(ROWS // 128):
            l = logits[m, 128 * i : 128 * (i + 1), :]
            parts = [l[:, 128 * k : 128 * (k + 1)] for k in range(COLS // 128)]
            lane_peak = functools.reduce(jnp.maximum, parts)
            lane_total = functools.reduce(jnp.add, [jnp.exp(p - lane_peak) for p in parts])
            lane_peak, lane_total = lane_peak.T, lane_total.T
            row_peak = jnp.max(lane_peak, axis=0, keepdims=True)
            row_total = jnp.sum(lane_total * jnp.exp(lane_peak - row_peak), axis=0, keepdims=True)
            row_lse.append(row_peak + jnp.log(row_total))
            l = l.reshape(16, 8, COLS)
            now = jnp.maximum(peak, jnp.max(l, axis=0))
            total = total * jnp.exp(peak - now) + jnp.sum(jnp.exp(l - now[None]), axis=0)
            peak = now
        col_peak = jnp.max(peak, axis=0, keepdims=True)
        col_lse = col_peak + jnp.log(jnp.sum(total * jnp.exp(peak - col_peak), axis=0, keepdims=True))
        parts = [col_lse[:, 128 * i : 128 * (i + 1)] for i in range(COLS // 128)]
        rest = [jnp.zeros((4, 128), F32)]
        cstat[m, col_me] = jnp.concatenate(parts + rest, axis=0)
        rstat[m, row_me] = jnp.concatenate(row_lse + rest, axis=0)

    def stat_copies(m, j):
        return [
            pltpu.make_async_remote_copy(
                src_ref=ref.at[m, me], dst_ref=ref.at[m, me], send_sem=stsem.at[m, kind, j], recv_sem=sem.at[m, me],
                device_id=peer(j)[1], device_id_type=MESH,
            )
            for kind, (ref, sem, me, peer) in enumerate(
                ((rstat, rssem, row_me, row_peer), (cstat, cssem, col_me, col_peer))
            )
        ]

    def stats_start(m):
        for j in FAR_FIRST:
            for c in stat_copies(m, j):
                c.start()

    def joined(all_):
        peak = jnp.max(all_, axis=0)
        return peak + jnp.log(jnp.sum(jnp.exp(all_ - peak[None]), axis=0))

    def stats_end(m):
        @pl.loop(1, 16)
        def _(j):
            arrived(rstat.at[m, row_peer(j)[0]], rssem.at[m, row_peer(j)[0]])
            arrived(cstat.at[m, col_peer(j)[0]], cssem.at[m, col_peer(j)[0]])

        stat[...] = joined(cstat[m])
        turned = jnp.concatenate([joined(rstat[m]), jnp.zeros((120, 128), F32)], axis=0).T
        for i in range(ROWS // 128):
            rcol[m, 128 * i : 128 * (i + 1), :] = jnp.broadcast_to(turned[:, i : i + 1], (128, 128))
        return jnp.concatenate([stat[i : i + 1, :] for i in range(COLS // 128)], axis=1)

    def chances(m, block, col_lse):
        l = logits[m, block, :]
        r = jnp.concatenate([rcol[m, block, :]] * (COLS // 128), axis=1)
        return jnp.exp(l - r) + jnp.exp(l - col_lse)

    tile(0)
    z_rest(1)
    local_stats(0)
    stats_start(0)
    complete(1)
    tile(1)
    local_stats(1)
    stats_start(1)
    teacher_lse = stats_end(0)

    @pl.loop(0, ROWS // 128)
    def _(i):
        block = pl.ds(pl.multiple_of(i * 128, 128), 128)
        logits[0, block, :] = chances(0, block, teacher_lse)

    student_lse = stats_end(1)

    @pl.loop(0, ROWS // 128)
    def _(i):
        block = pl.ds(pl.multiple_of(i * 128, 128), 128)
        c = 0.5 * (chances(1, block, student_lse) - logits[0, block, :])
        cpl[block, :] = c.astype(BF16)
        cplt[:, block] = c.T.astype(BF16)

    for m in (0, 1):

        @pl.loop(1, 16)
        def _(j):
            for c in stat_copies(m, j):
                c.wait_send()

    factor = scale[1]

    def text_dot(ya, yb):
        a = jnp.concatenate([cplt[pl.ds(pl.multiple_of(k * 128, 128), 128), :] for k in (ya, yb)], axis=0)
        return factor * jnp.dot(a, rows[1], preferred_element_type=F32)

    def image_dot(first):
        parts = [mod(z + first + k, NZ) for k in range(4)]
        a = jnp.concatenate([cpl[pl.ds(pl.multiple_of(k * N, N), N), :] for k in parts], axis=0)
        return factor * jnp.dot(a, cols[1], preferred_element_type=F32)

    def text_send(k, dst, sem, to):
        send(tsend.at[pl.ds(k * N, N)], dst, sem, to)

    far = text_dot(y2, yu)
    tsend[0:128, :] = far[0:128].astype(BF16)
    text_send(0, arecv.at[0], asem.at[0], up_y)
    text_send(1, arecv.at[1], asem.at[1], down_y)
    tsend[192:256, :] = far[192:256].astype(BF16)
    text_send(3, brecv.at[1], bsem.at[1], up_y)
    tacc[128:192, :] = far[128:192]
    first = 4 * mod(core + g, 2)
    isend[...] = image_dot(4 - first).astype(BF16)
    send(isend, irecv, isem.at[0], sibling)
    close = text_dot(yd, y)
    tsend[256:320, :] = close[0:64].astype(BF16)
    text_send(4, brecv.at[2], bsem.at[2], down_y)
    tacc[320:512, :] = close[64:256]
    iown[...] = image_dot(first)
    arrived(irecv, isem.at[0])
    mine_too = jnp.logical_or(g == 1, core == 1)
    down = div(first, 4)
    toward = device(xh, g, y, mod(z + 1 + 6 * down, NZ), core)

    def image_part(k):
        return pl.ds(pl.multiple_of(k * N, N), N)

    def image_sum(k):
        summed = iown[image_part(k), :] + irecv[image_part(k), :].astype(F32)
        iown[image_part(k), :] = summed
        zsend[image_part(k), :] = summed.astype(BF16)

    def image_send(k, when=None):
        to = device(xh, 0, y, mod(z + first + k, NZ), g)
        send(zsend.at[image_part(k)], zrecv.at[z], zsem.at[z], to, when)

    image_sum(3 - 2 * down)
    send(zsend.at[image_part(3 - 2 * down)], crecv, tosem.at[0], toward)
    image_sum(0)
    image_send(0, mine_too)
    image_sum(1 + 2 * down)
    image_send(1 + 2 * down)
    iown[image_part(2), :] = iown[image_part(2), :] + irecv[image_part(2), :].astype(F32)
    arrived(arecv.at[0], asem.at[0])
    tsend[128:192, :] = (tacc[128:192, :] + arecv[0].astype(F32)).astype(BF16)
    text_send(2, brecv.at[0], bsem.at[0], up_y)
    arrived(arecv.at[1], asem.at[1])
    tsend[320:384, :] = (tacc[320:384, :] + arecv[1].astype(F32)).astype(BF16)
    text_send(5, brecv.at[3], bsem.at[3], down_y)
    arrived(crecv, tosem.at[0])
    zsend[image_part(2), :] = (iown[image_part(2), :] + crecv[...].astype(F32)).astype(BF16)
    image_send(2)
    for k in (1, 2, 0, 3):
        arrived(brecv.at[k], bsem.at[k])
    for k in (0, 1):
        part = slice(384 + k * N, 384 + (k + 1) * N)
        total = tacc[part, :] + (brecv[k].astype(F32) + brecv[2 + k].astype(F32))
        tacc[part, :] = total
        xsend[k * N : (k + 1) * N, :] = total.astype(BF16)
        send(xsend.at[pl.ds(k * N, N)], xrecv.at[x], xsem.at[x], device(k, 1, y, z, core), x != 2 * k + 1)

    def received(k):
        arrived(zrecv.at[k], zsem.at[k])
        return zrecv[k].astype(F32)

    @pl.when(g == 0)
    def _():
        acc = received(mod(z + 1, NZ))
        for j in (7, 4, 2, 6):
            acc = acc + received(mod(z + j, NZ))
        tacc[0:N, :] = acc

    @pl.when(jnp.logical_and(g == 0, core == 0))
    def _():
        out[0] = tacc[0:N, :] + iown[0:N, :]

    @pl.when(jnp.logical_and(g == 0, core == 1))
    def _():
        out[0] = tacc[0:N, :] + received(z)

    @pl.when(g == 1)
    def _():
        acc = tacc[pl.ds(pl.multiple_of(384 + xh * N, N), N), :]
        for j in range(1, NX):
            k = mod(x + j, NX)
            arrived(xrecv.at[k], xsem.at[k])
            acc = acc + xrecv[k].astype(F32)
        out[0] = acc

    finish()


def per_device(teacher_image, teacher_text, student_image, student_text, scales):
    shard, width = teacher_image.shape
    assert shard == N
    dma = pltpu.SemaphoreType.DMA
    vmem = pltpu.VMEM
    teacher_image, teacher_text, student_image, student_text, scales = [
        pltpu.with_memory_space_constraint(a, pltpu.HBM)
        for a in (teacher_image, teacher_text, student_image, student_text, scales)
    ]
    any_ = pl.BlockSpec(memory_space=pltpu.HBM)
    return pl.pallas_call(
        kernel,
        out_shape=jax.ShapeDtypeStruct((1, N, width), F32),
        in_specs=[any_] * 5,
        out_specs=pl.BlockSpec(memory_space=pltpu.VMEM),
        scratch_shapes=[
            vmem((2, ROWS, width), BF16),
            vmem((2, COLS, width), BF16),
            vmem((2, ROWS, COLS), F32),
            vmem((8, 128), F32),
            vmem((2, NZ * NC, 8, 128), F32),
            vmem((2, NX * NY, 8, 128), F32),
            vmem((2, ROWS, 128), F32),
            vmem((ROWS, COLS), BF16),
            vmem((COLS, ROWS), BF16),
            vmem((COLS, width), F32),
            vmem((384, width), BF16),
            vmem((2, N, width), BF16),
            vmem((4, N, width), BF16),
            vmem((128, width), BF16),
            vmem((NX, N, width), BF16),
            vmem((256, width), BF16),
            vmem((256, width), F32),
            vmem((256, width), BF16),
            vmem((256, width), BF16),
            vmem((NZ, N, width), BF16),
            vmem((N, width), BF16),
            pltpu.SMEM((2,), F32),
            dma((5,)),
            dma((SENDS,)),
            dma((2, 2, 16)),
            dma((2, NZ)),
            dma((2, 2 * NY)),
            dma((2, NZ * NC)),
            dma((2, NX * NY)),
            dma((2,)),
            dma((4,)),
            dma((NX,)),
            dma((1,)),
            dma((NZ,)),
            dma((1,)),
        ],
        compiler_params=pltpu.CompilerParams(
            collective_id=0, has_side_effects=True, vmem_limit_bytes=48 * 2**20
        ),
    )(teacher_image, teacher_text, student_image, student_text, scales)


def solution(mesh):
    assert mesh.shape["group"] == 2 and mesh.shape["batch"] == 2 * NY * NZ * NC
    return jax.shard_map(
        per_device,
        mesh=mesh,
        in_specs=(P("batch", None), P("batch", None), P("batch", None), P("batch", None), P()),
        out_specs=P("group", "batch", None),
        check_vma=False,
    )
```

```python
import functools

import jax
import jax.numpy as jnp
from jax import lax
from jax.experimental import pallas as pl
from jax.experimental.pallas import tpu as pltpu
from jax.sharding import PartitionSpec as P

MESH = pl.DeviceIdType.MESH
F32 = jnp.float32
BF16 = jnp.bfloat16
NX, NY, NZ, NC = 4, 4, 8, 2
N = 64
ROWS = NZ * N
COLS = NY * 2 * N
SENDS = 80
FAR_FIRST = (8, 9, 7, 6, 10, 5, 11, 4, 12, 3, 13, 2, 14, 1, 15)


def mod(a, n):
    return lax.rem(a, jnp.int32(n))


def div(a, n):
    return lax.div(a, jnp.int32(n))


def device(x_hi, x_lo, y, z, core):
    return {"group": x_lo, "batch": ((x_hi * NZ + z) * NY + y) * NC + core}


def kernel(
    ti, tt, si, st, scales, out,
    rows, cols, logits, stat, rstat, cstat, rcol, cpl, cplt,
    tacc, tsend, arecv, brecv, xsend, xrecv, isend, iown, irecv, zsend, zrecv, crecv, scale,
    lsem, ssem, stsem, rsem, csem, rssem, cssem, asem, bsem, xsem, isem, zsem, tosem,
):
    b = lax.axis_index("batch")
    g = lax.axis_index("group")
    core, y, z, xh = mod(b, NC), mod(div(b, NC), NY), mod(div(b, NC * NY), NZ), div(b, NC * NY * NZ)
    x = 2 * xh + g
    other = 1 - core
    step = 1 - 2 * core
    yu, yd, y2 = mod(y + 1, NY), mod(y + 3, NY), mod(y + 2, NY)
    source = core == g

    sibling = device(xh, g, y, z, other)
    up_y, down_y = device(xh, g, yu, z, core), device(xh, g, yd, z, core)
    across = device(1 - xh, 1 - g, y, z, core)
    beside = device(xh, 1 - g, y, z, core)

    pending = []

    def copy(src, dst, sem, to):
        k = len(pending)
        c = pltpu.make_async_remote_copy(
            src_ref=src, dst_ref=dst, send_sem=ssem.at[k], recv_sem=sem, device_id=to, device_id_type=MESH
        )
        return c

    def send(src, dst, sem, to, when=None):
        c = copy(src, dst, sem, to)
        pending.append((c, when))
        if when is None:
            c.start()
        else:
            pl.when(when)(c.start)

    def finish():
        assert len(pending) < SENDS
        for entry in pending:
            if entry is not None:
                c, when = entry
                if when is None:
                    c.wait_send()
                else:
                    pl.when(when)(c.wait_send)

    def arrived(dst, sem):
        pltpu.make_async_remote_copy(
            src_ref=dst, dst_ref=dst, send_sem=ssem.at[SENDS - 1], recv_sem=sem, device_id=sibling, device_id_type=MESH
        ).wait_recv()

    def row_at(m, k):
        return rows.at[m, pl.ds(pl.multiple_of(k * N, N), N)]

    def col_slot(yy, hi):
        return yy * 2 + hi

    def col_at(m, k):
        return cols.at[m, pl.ds(pl.multiple_of(k * N, N), N)]

    row_me, col_me = z * NC + core, x * NY + y

    def row_peer(j):
        q = mod(row_me + j, NZ * NC)
        return q, device(xh, g, y, div(q, NC), mod(q, NC))

    def col_peer(j):
        q = mod(col_me + j, NX * NY)
        qx = div(q, NY)
        return q, device(div(qx, 2), mod(qx, 2), mod(q, NY), z, core)

    barrier = pltpu.get_barrier_semaphore()

    near = [sibling, up_y, down_y, device(xh, g, y2, z, core), across, beside]
    near += [device(xh, g, y, mod(z + d, NZ), c) for d in (1, 7, 2, 6) for c in (0, 1)]
    for to in near:
        pl.semaphore_signal(barrier, inc=1, device_id=to, device_id_type=MESH)

    mine = col_slot(y, xh)
    locals_ = [
        pltpu.make_async_copy(tt, col_at(0, mine), lsem.at[0]),
        pltpu.make_async_copy(st, col_at(1, mine), lsem.at[1]),
        pltpu.make_async_copy(scales, scale, lsem.at[4]),
    ]
    row_locals = [
        pltpu.make_async_copy(ti, row_at(0, z), lsem.at[2]),
        pltpu.make_async_copy(si, row_at(1, z), lsem.at[3]),
    ]
    for c in locals_:
        c.start()

    @pl.when(source)
    def _():
        for c in row_locals:
            c.start()

    pl.semaphore_wait(barrier, len(near))
    def send_col(m, k, to):
        src = (tt, st)[m] if k is mine else col_at(m, k)
        send(src, col_at(m, k), csem.at[m, k], to)

    def send_row(m, k, to, when=None):
        src = (ti, si)[m] if k is z else row_at(m, k)
        send(src, row_at(m, k), rsem.at[m, k], to, when)

    def got_col(m, k):
        arrived(col_at(m, k), csem.at[m, k])

    def got_row(m, k):
        arrived(row_at(m, k), rsem.at[m, k])

    def z_from(d):
        return mod(z - step * d + NZ, NZ)

    def z_start(m, d):
        send_row(m, z, device(xh, g, y, mod(z + d, NZ), 0), source)
        send_row(m, z, device(xh, g, y, mod(z + NZ - d, NZ), 1), source)

    def z_own(m):
        z_start(m, 2)
        z_start(m, 1)
        send_row(m, z, sibling, source)

    def z_pass(m):
        k = z_from(2)
        got_row(m, k)
        send_row(m, k, device(xh, g, y, mod(z + 2 * step + NZ, NZ), core), core == m)
        send_row(m, k, device(xh, g, y, mod(z + step + NZ, NZ), core))
        send_row(m, k, sibling)

    def y_start(m):
        send_col(m, mine, device(xh, g, y2, z, core))
        send_col(m, mine, up_y)
        send_col(m, mine, down_y)

    def x_pass(m):
        k = col_slot(y, 1 - xh)
        got_col(m, k)
        send_col(m, k, up_y)
        send_col(m, k, down_y)

    def y_pass(m):
        k = col_slot(y2, xh)
        got_col(m, k)
        send_col(m, k, across)

    def z_rest(m):
        got_row(m, z_from(1))
        send_row(m, z_from(1), sibling)
        far = z_from(4)

        @pl.when(core == m)
        def _():
            got_row(m, far)

        send_row(m, far, sibling, core == m)
        got_row(m, z_from(3))
        send_row(m, z_from(3), sibling)

    def complete(m):
        for yy in (yu, yd):
            got_col(m, col_slot(yy, xh))
            got_col(m, col_slot(yy, 1 - xh))
        got_col(m, col_slot(y2, 1 - xh))
        for d in (1, 2, 3):
            got_row(m, mod(z + step * d + NZ, NZ))

        @pl.when(core != m)
        def _():
            got_row(m, mod(z + 4, NZ))

        @pl.when(jnp.logical_not(source))
        def _():
            got_row(m, z)

    send_col(0, mine, across)
    z_start(0, 2)
    y_start(0)
    z_start(0, 1)
    send_row(0, z, sibling, source)
    send_col(1, mine, across)
    y_start(1)
    z_start(1, 2)
    z_start(1, 1)
    send_row(1, z, sibling, source)
    x_pass(0)
    z_pass(0)
    y_pass(0)
    x_pass(1)
    z_pass(1)
    y_pass(1)
    z_rest(0)
    complete(0)
    for c in locals_:
        c.wait()

    @pl.when(source)
    def _():
        for c in row_locals:
            c.wait()

    def tile(m):
        factor = scale[m]

        logits[m] = factor * lax.dot_general(
            rows[m], cols[m], (((1,), (1,)), ((), ())), preferred_element_type=F32
        )

    def local_stats(m):
        peak, total = jnp.full((8, COLS), -3.0e38, F32), jnp.zeros((8, COLS), F32)
        row_lse = []
        for i in range(ROWS // 128):
            l = logits[m, 128 * i : 128 * (i + 1), :]
            parts = [l[:, 128 * k : 128 * (k + 1)] for k in range(COLS // 128)]
            lane_peak = functools.reduce(jnp.maximum, parts)
            lane_total = functools.reduce(jnp.add, [jnp.exp(p - lane_peak) for p in parts])
            lane_peak, lane_total = lane_peak.T, lane_total.T
            row_peak = jnp.max(lane_peak, axis=0, keepdims=True)
            row_total = jnp.sum(lane_total * jnp.exp(lane_peak - row_peak), axis=0, keepdims=True)
            row_lse.append(row_peak + jnp.log(row_total))
            l = l.reshape(16, 8, COLS)
            now = jnp.maximum(peak, jnp.max(l, axis=0))
            total = total * jnp.exp(peak - now) + jnp.sum(jnp.exp(l - now[None]), axis=0)
            peak = now
        col_peak = jnp.max(peak, axis=0, keepdims=True)
        col_lse = col_peak + jnp.log(jnp.sum(total * jnp.exp(peak - col_peak), axis=0, keepdims=True))
        parts = [col_lse[:, 128 * i : 128 * (i + 1)] for i in range(COLS // 128)]
        rest = [jnp.zeros((4, 128), F32)]
        cstat[m, col_me] = jnp.concatenate(parts + rest, axis=0)
        rstat[m, row_me] = jnp.concatenate(row_lse + rest, axis=0)

    def stat_copies(m, j):
        return [
            pltpu.make_async_remote_copy(
                src_ref=ref.at[m, me], dst_ref=ref.at[m, me], send_sem=stsem.at[m, kind, j], recv_sem=sem.at[m, me],
                device_id=peer(j)[1], device_id_type=MESH,
            )
            for kind, (ref, sem, me, peer) in enumerate(
                ((rstat, rssem, row_me, row_peer), (cstat, cssem, col_me, col_peer))
            )
        ]

    def stats_start(m):
        for j in FAR_FIRST:
            for c in stat_copies(m, j):
                c.start()

    def joined(all_):
        peak = jnp.max(all_, axis=0)
        return peak + jnp.log(jnp.sum(jnp.exp(all_ - peak[None]), axis=0))

    def stats_end(m):
        @pl.loop(1, 16)
        def _(j):
            arrived(rstat.at[m, row_peer(j)[0]], rssem.at[m, row_peer(j)[0]])
            arrived(cstat.at[m, col_peer(j)[0]], cssem.at[m, col_peer(j)[0]])

        stat[...] = joined(cstat[m])
        turned = jnp.concatenate([joined(rstat[m]), jnp.zeros((120, 128), F32)], axis=0).T
        for i in range(ROWS // 128):
            rcol[m, 128 * i : 128 * (i + 1), :] = jnp.broadcast_to(turned[:, i : i + 1], (128, 128))
        return jnp.concatenate([stat[i : i + 1, :] for i in range(COLS // 128)], axis=1)

    def chances(m, block, col_lse):
        l = logits[m, block, :]
        r = jnp.concatenate([rcol[m, block, :]] * (COLS // 128), axis=1)
        return jnp.exp(l - r) + jnp.exp(l - col_lse)

    tile(0)
    z_rest(1)
    local_stats(0)
    stats_start(0)
    complete(1)
    tile(1)
    local_stats(1)
    stats_start(1)
    teacher_lse = stats_end(0)

    @pl.loop(0, ROWS // 128)
    def _(i):
        block = pl.ds(pl.multiple_of(i * 128, 128), 128)
        logits[0, block, :] = chances(0, block, teacher_lse)

    student_lse = stats_end(1)

    @pl.loop(0, ROWS // 128)
    def _(i):
        block = pl.ds(pl.multiple_of(i * 128, 128), 128)
        c = 0.5 * (chances(1, block, student_lse) - logits[0, block, :])
        cpl[block, :] = c.astype(BF16)
        cplt[:, block] = c.T.astype(BF16)

    for m in (0, 1):

        @pl.loop(1, 16)
        def _(j):
            for c in stat_copies(m, j):
                c.wait_send()

    factor = scale[1]

    def text_dot(ya, yb):
        a = jnp.concatenate([cplt[pl.ds(pl.multiple_of(k * 128, 128), 128), :] for k in (ya, yb)], axis=0)
        return factor * jnp.dot(a, rows[1], preferred_element_type=F32)

    def image_dot(first):
        parts = [mod(z + first + k, NZ) for k in range(4)]
        a = jnp.concatenate([cpl[pl.ds(pl.multiple_of(k * N, N), N), :] for k in parts], axis=0)
        return factor * jnp.dot(a, cols[1], preferred_element_type=F32)

    def text_send(k, dst, sem, to):
        send(tsend.at[pl.ds(k * N, N)], dst, sem, to)

    far = text_dot(y2, yu)
    tsend[0:128, :] = far[0:128].astype(BF16)
    text_send(0, arecv.at[0], asem.at[0], up_y)
    text_send(1, arecv.at[1], asem.at[1], down_y)
    tsend[192:256, :] = far[192:256].astype(BF16)
    text_send(3, brecv.at[1], bsem.at[1], up_y)
    tacc[128:192, :] = far[128:192]
    first = 4 * mod(core + g, 2)
    isend[...] = image_dot(4 - first).astype(BF16)
    send(isend, irecv, isem.at[0], sibling)
    close = text_dot(yd, y)
    tsend[256:320, :] = close[0:64].astype(BF16)
    text_send(4, brecv.at[2], bsem.at[2], down_y)
    tacc[320:512, :] = close[64:256]
    iown[...] = image_dot(first)
    arrived(irecv, isem.at[0])
    mine_too = jnp.logical_or(g == 1, core == 1)
    down = div(first, 4)
    toward = device(xh, g, y, mod(z + 1 + 6 * down, NZ), core)

    def image_part(k):
        return pl.ds(pl.multiple_of(k * N, N), N)

    def image_sum(k):
        summed = iown[image_part(k), :] + irecv[image_part(k), :].astype(F32)
        iown[image_part(k), :] = summed
        zsend[image_part(k), :] = summed.astype(BF16)

    def image_send(k, when=None):
        to = device(xh, 0, y, mod(z + first + k, NZ), g)
        send(zsend.at[image_part(k)], zrecv.at[z], zsem.at[z], to, when)

    image_sum(3 - 2 * down)
    send(zsend.at[image_part(3 - 2 * down)], crecv, tosem.at[0], toward)
    image_sum(0)
    image_send(0, mine_too)
    image_sum(1 + 2 * down)
    image_send(1 + 2 * down)
    iown[image_part(2), :] = iown[image_part(2), :] + irecv[image_part(2), :].astype(F32)
    arrived(arecv.at[0], asem.at[0])
    tsend[128:192, :] = (tacc[128:192, :] + arecv[0].astype(F32)).astype(BF16)
    text_send(2, brecv.at[0], bsem.at[0], up_y)
    arrived(arecv.at[1], asem.at[1])
    tsend[320:384, :] = (tacc[320:384, :] + arecv[1].astype(F32)).astype(BF16)
    text_send(5, brecv.at[3], bsem.at[3], down_y)
    arrived(crecv, tosem.at[0])
    zsend[image_part(2), :] = (iown[image_part(2), :] + crecv[...].astype(F32)).astype(BF16)
    image_send(2)
    for k in (1, 2, 0, 3):
        arrived(brecv.at[k], bsem.at[k])
    for k in (0, 1):
        part = slice(384 + k * N, 384 + (k + 1) * N)
        total = tacc[part, :] + (brecv[k].astype(F32) + brecv[2 + k].astype(F32))
        tacc[part, :] = total
        xsend[k * N : (k + 1) * N, :] = total.astype(BF16)
        send(xsend.at[pl.ds(k * N, N)], xrecv.at[x], xsem.at[x], device(k, 1, y, z, core), x != 2 * k + 1)

    def received(k):
        arrived(zrecv.at[k], zsem.at[k])
        return zrecv[k].astype(F32)

    @pl.when(g == 0)
    def _():
        acc = received(mod(z + 1, NZ))
        for j in (7, 4, 2, 6):
            acc = acc + received(mod(z + j, NZ))
        tacc[0:N, :] = acc

    @pl.when(jnp.logical_and(g == 0, core == 0))
    def _():
        out[0] = tacc[0:N, :] + iown[0:N, :]

    @pl.when(jnp.logical_and(g == 0, core == 1))
    def _():
        out[0] = tacc[0:N, :] + received(z)

    @pl.when(g == 1)
    def _():
        acc = tacc[pl.ds(pl.multiple_of(384 + xh * N, N), N), :]
        for j in range(1, NX):
            k = mod(x + j, NX)
            arrived(xrecv.at[k], xsem.at[k])
            acc = acc + xrecv[k].astype(F32)
        out[0] = acc

    finish()


def per_device(teacher_image, teacher_text, student_image, student_text, scales):
    shard, width = teacher_image.shape
    assert shard == N
    dma = pltpu.SemaphoreType.DMA
    vmem = pltpu.VMEM
    teacher_image, teacher_text, student_image, student_text, scales = [
        pltpu.with_memory_space_constraint(a, pltpu.HBM)
        for a in (teacher_image, teacher_text, student_image, student_text, scales)
    ]
    any_ = pl.BlockSpec(memory_space=pltpu.HBM)
    return pl.pallas_call(
        kernel,
        out_shape=jax.ShapeDtypeStruct((1, N, width), F32),
        in_specs=[any_] * 5,
        out_specs=pl.BlockSpec(memory_space=pltpu.VMEM),
        scratch_shapes=[
            vmem((2, ROWS, width), BF16),
            vmem((2, COLS, width), BF16),
            vmem((2, ROWS, COLS), F32),
            vmem((8, 128), F32),
            vmem((2, NZ * NC, 8, 128), F32),
            vmem((2, NX * NY, 8, 128), F32),
            vmem((2, ROWS, 128), F32),
            vmem((ROWS, COLS), BF16),
            vmem((COLS, ROWS), BF16),
            vmem((COLS, width), F32),
            vmem((384, width), BF16),
            vmem((2, N, width), BF16),
            vmem((4, N, width), BF16),
            vmem((128, width), BF16),
            vmem((NX, N, width), BF16),
            vmem((256, width), BF16),
            vmem((256, width), F32),
            vmem((256, width), BF16),
            vmem((256, width), BF16),
            vmem((NZ, N, width), BF16),
            vmem((N, width), BF16),
            pltpu.SMEM((2,), F32),
            dma((5,)),
            dma((SENDS,)),
            dma((2, 2, 16)),
            dma((2, NZ)),
            dma((2, 2 * NY)),
            dma((2, NZ * NC)),
            dma((2, NX * NY)),
            dma((2,)),
            dma((4,)),
            dma((NX,)),
            dma((1,)),
            dma((NZ,)),
            dma((1,)),
        ],
        compiler_params=pltpu.CompilerParams(
            collective_id=0, has_side_effects=True, vmem_limit_bytes=48 * 2**20
        ),
    )(teacher_image, teacher_text, student_image, student_text, scales)


def solution(mesh):
    assert mesh.shape["group"] == 2 and mesh.shape["batch"] == 2 * NY * NZ * NC
    return jax.shard_map(
        per_device,
        mesh=mesh,
        in_specs=(P("batch", None), P("batch", None), P("batch", None), P("batch", None), P()),
        out_specs=P("group", "batch", None),
        check_vma=False,
    )
```

```python
import functools

import jax
import jax.numpy as jnp
from jax import lax
from jax.experimental import pallas as pl
from jax.experimental.pallas import tpu as pltpu
from jax.sharding import PartitionSpec as P

MESH = pl.DeviceIdType.MESH
F32 = jnp.float32
BF16 = jnp.bfloat16
NX, NY, NZ, NC = 4, 4, 8, 2
N = 64
ROWS = NZ * N
COLS = NY * 2 * N
SENDS = 80
FAR_FIRST = (8, 9, 7, 6, 10, 5, 11, 4, 12, 3, 13, 2, 14, 1, 15)


def mod(a, n):
    return lax.rem(a, jnp.int32(n))


def div(a, n):
    return lax.div(a, jnp.int32(n))


def device(x_hi, x_lo, y, z, core):
    return {"group": x_lo, "batch": ((x_hi * NZ + z) * NY + y) * NC + core}


def kernel(
    ti, tt, si, st, scales, out,
    rows, cols, logits, stat, rstat, cstat, rcol, cpl, cplt,
    tacc, tsend, arecv, brecv, xsend, xrecv, isend, iown, irecv, zsend, zrecv, crecv, scale,
    lsem, ssem, stsem, rsem, csem, rssem, cssem, asem, bsem, xsem, isem, zsem, tosem,
):
    b = lax.axis_index("batch")
    g = lax.axis_index("group")
    core, y, z, xh = mod(b, NC), mod(div(b, NC), NY), mod(div(b, NC * NY), NZ), div(b, NC * NY * NZ)
    x = 2 * xh + g
    other = 1 - core
    step = 1 - 2 * core
    yu, yd, y2 = mod(y + 1, NY), mod(y + 3, NY), mod(y + 2, NY)
    source = core == g

    sibling = device(xh, g, y, z, other)
    up_y, down_y = device(xh, g, yu, z, core), device(xh, g, yd, z, core)
    across = device(1 - xh, 1 - g, y, z, core)
    beside = device(xh, 1 - g, y, z, core)

    pending = []

    def copy(src, dst, sem, to):
        k = len(pending)
        c = pltpu.make_async_remote_copy(
            src_ref=src, dst_ref=dst, send_sem=ssem.at[k], recv_sem=sem, device_id=to, device_id_type=MESH
        )
        return c

    def send(src, dst, sem, to, when=None):
        c = copy(src, dst, sem, to)
        pending.append((c, when))
        if when is None:
            c.start()
        else:
            pl.when(when)(c.start)

    def finish():
        assert len(pending) < SENDS
        for entry in pending:
            if entry is not None:
                c, when = entry
                if when is None:
                    c.wait_send()
                else:
                    pl.when(when)(c.wait_send)

    def arrived(dst, sem):
        pltpu.make_async_remote_copy(
            src_ref=dst, dst_ref=dst, send_sem=ssem.at[SENDS - 1], recv_sem=sem, device_id=sibling, device_id_type=MESH
        ).wait_recv()

    def row_at(m, k):
        return rows.at[m, pl.ds(pl.multiple_of(k * N, N), N)]

    def col_slot(yy, hi):
        return yy * 2 + hi

    def col_at(m, k):
        return cols.at[m, pl.ds(pl.multiple_of(k * N, N), N)]

    row_me, col_me = z * NC + core, x * NY + y

    def row_peer(j):
        q = mod(row_me + j, NZ * NC)
        return q, device(xh, g, y, div(q, NC), mod(q, NC))

    def col_peer(j):
        q = mod(col_me + j, NX * NY)
        qx = div(q, NY)
        return q, device(div(qx, 2), mod(qx, 2), mod(q, NY), z, core)

    barrier = pltpu.get_barrier_semaphore()

    near = [device(xh, g, y, mod(z + d, NZ), c) for d in (2, 6) for c in (0, 1)]
    near += [device(xh, g, y2, z, core)]
    near += [device(xh, g, y, mod(z + d, NZ), c) for d in (1, 7) for c in (0, 1)]
    near += [across, up_y, down_y, beside, sibling]
    for to in near:
        pl.semaphore_signal(barrier, inc=1, device_id=to, device_id_type=MESH)

    mine = col_slot(y, xh)
    locals_ = [
        pltpu.make_async_copy(tt, col_at(0, mine), lsem.at[0]),
        pltpu.make_async_copy(st, col_at(1, mine), lsem.at[1]),
        pltpu.make_async_copy(scales, scale, lsem.at[4]),
    ]
    row_locals = [
        pltpu.make_async_copy(ti, row_at(0, z), lsem.at[2]),
        pltpu.make_async_copy(si, row_at(1, z), lsem.at[3]),
    ]
    for c in locals_:
        c.start()

    @pl.when(source)
    def _():
        for c in row_locals:
            c.start()

    pl.semaphore_wait(barrier, len(near))
    def send_col(m, k, to):
        src = (tt, st)[m] if k is mine else col_at(m, k)
        send(src, col_at(m, k), csem.at[m, k], to)

    def send_row(m, k, to, when=None):
        src = (ti, si)[m] if k is z else row_at(m, k)
        send(src, row_at(m, k), rsem.at[m, k], to, when)

    def got_col(m, k):
        arrived(col_at(m, k), csem.at[m, k])

    def got_row(m, k):
        arrived(row_at(m, k), rsem.at[m, k])

    def z_from(d):
        return mod(z - step * d + NZ, NZ)

    def z_start(m, d):
        send_row(m, z, device(xh, g, y, mod(z + d, NZ), 0), source)
        send_row(m, z, device(xh, g, y, mod(z + NZ - d, NZ), 1), source)

    def z_own(m):
        z_start(m, 2)
        z_start(m, 1)
        send_row(m, z, sibling, source)

    def z_pass(m):
        k = z_from(2)
        got_row(m, k)
        send_row(m, k, device(xh, g, y, mod(z + 2 * step + NZ, NZ), core), core == m)
        send_row(m, k, device(xh, g, y, mod(z + step + NZ, NZ), core))
        send_row(m, k, sibling)

    def y_start(m):
        send_col(m, mine, device(xh, g, y2, z, core))
        send_col(m, mine, up_y)
        send_col(m, mine, down_y)

    def x_pass(m):
        k = col_slot(y, 1 - xh)
        got_col(m, k)
        send_col(m, k, up_y)
        send_col(m, k, down_y)

    def y_pass(m):
        k = col_slot(y2, xh)
        got_col(m, k)
        send_col(m, k, across)

    def z_rest(m):
        got_row(m, z_from(1))
        send_row(m, z_from(1), sibling)
        far = z_from(4)

        @pl.when(core == m)
        def _():
            got_row(m, far)

        send_row(m, far, sibling, core == m)
        got_row(m, z_from(3))
        send_row(m, z_from(3), sibling)

    def complete(m):
        for yy in (yu, yd):
            got_col(m, col_slot(yy, xh))
            got_col(m, col_slot(yy, 1 - xh))
        got_col(m, col_slot(y2, 1 - xh))
        for d in (1, 2, 3):
            got_row(m, mod(z + step * d + NZ, NZ))

        @pl.when(core != m)
        def _():
            got_row(m, mod(z + 4, NZ))

        @pl.when(jnp.logical_not(source))
        def _():
            got_row(m, z)

    send_col(0, mine, across)
    z_start(0, 2)
    y_start(0)
    z_start(0, 1)
    send_row(0, z, sibling, source)
    send_col(1, mine, across)
    y_start(1)
    z_start(1, 2)
    z_start(1, 1)
    send_row(1, z, sibling, source)
    x_pass(0)
    z_pass(0)
    y_pass(0)
    x_pass(1)
    z_pass(1)
    y_pass(1)
    z_rest(0)
    complete(0)
    for c in locals_:
        c.wait()

    @pl.when(source)
    def _():
        for c in row_locals:
            c.wait()

    def tile(m):
        factor = scale[m]

        logits[m] = factor * lax.dot_general(
            rows[m], cols[m], (((1,), (1,)), ((), ())), preferred_element_type=F32
        )

    def local_stats(m):
        peak, total = jnp.full((8, COLS), -3.0e38, F32), jnp.zeros((8, COLS), F32)
        row_lse = []
        for i in range(ROWS // 128):
            l = logits[m, 128 * i : 128 * (i + 1), :]
            parts = [l[:, 128 * k : 128 * (k + 1)] for k in range(COLS // 128)]
            lane_peak = functools.reduce(jnp.maximum, parts)
            lane_total = functools.reduce(jnp.add, [jnp.exp(p - lane_peak) for p in parts])
            lane_peak, lane_total = lane_peak.T, lane_total.T
            row_peak = jnp.max(lane_peak, axis=0, keepdims=True)
            row_total = jnp.sum(lane_total * jnp.exp(lane_peak - row_peak), axis=0, keepdims=True)
            row_lse.append(row_peak + jnp.log(row_total))
            l = l.reshape(16, 8, COLS)
            now = jnp.maximum(peak, jnp.max(l, axis=0))
            total = total * jnp.exp(peak - now) + jnp.sum(jnp.exp(l - now[None]), axis=0)
            peak = now
        col_peak = jnp.max(peak, axis=0, keepdims=True)
        col_lse = col_peak + jnp.log(jnp.sum(total * jnp.exp(peak - col_peak), axis=0, keepdims=True))
        parts = [col_lse[:, 128 * i : 128 * (i + 1)] for i in range(COLS // 128)]
        rest = [jnp.zeros((4, 128), F32)]
        cstat[m, col_me] = jnp.concatenate(parts + rest, axis=0)
        rstat[m, row_me] = jnp.concatenate(row_lse + rest, axis=0)

    def stat_copies(m, j):
        return [
            pltpu.make_async_remote_copy(
                src_ref=ref.at[m, me], dst_ref=ref.at[m, me], send_sem=stsem.at[m, kind, j], recv_sem=sem.at[m, me],
                device_id=peer(j)[1], device_id_type=MESH,
            )
            for kind, (ref, sem, me, peer) in enumerate(
                ((rstat, rssem, row_me, row_peer), (cstat, cssem, col_me, col_peer))
            )
        ]

    def stats_start(m):
        for j in FAR_FIRST:
            for c in stat_copies(m, j):
                c.start()

    def joined(all_):
        peak = jnp.max(all_, axis=0)
        return peak + jnp.log(jnp.sum(jnp.exp(all_ - peak[None]), axis=0))

    def stats_end(m):
        @pl.loop(1, 16)
        def _(j):
            arrived(rstat.at[m, row_peer(j)[0]], rssem.at[m, row_peer(j)[0]])
            arrived(cstat.at[m, col_peer(j)[0]], cssem.at[m, col_peer(j)[0]])

        stat[...] = joined(cstat[m])
        turned = jnp.concatenate([joined(rstat[m]), jnp.zeros((120, 128), F32)], axis=0).T
        for i in range(ROWS // 128):
            rcol[m, 128 * i : 128 * (i + 1), :] = jnp.broadcast_to(turned[:, i : i + 1], (128, 128))
        return jnp.concatenate([stat[i : i + 1, :] for i in range(COLS // 128)], axis=1)

    def chances(m, block, col_lse):
        l = logits[m, block, :]
        r = jnp.concatenate([rcol[m, block, :]] * (COLS // 128), axis=1)
        return jnp.exp(l - r) + jnp.exp(l - col_lse)

    tile(0)
    z_rest(1)
    local_stats(0)
    stats_start(0)
    complete(1)
    tile(1)
    local_stats(1)
    stats_start(1)
    teacher_lse = stats_end(0)

    @pl.loop(0, ROWS // 128)
    def _(i):
        block = pl.ds(pl.multiple_of(i * 128, 128), 128)
        logits[0, block, :] = chances(0, block, teacher_lse)

    student_lse = stats_end(1)

    @pl.loop(0, ROWS // 128)
    def _(i):
        block = pl.ds(pl.multiple_of(i * 128, 128), 128)
        c = 0.5 * (chances(1, block, student_lse) - logits[0, block, :])
        cpl[block, :] = c.astype(BF16)
        cplt[:, block] = c.T.astype(BF16)

    for m in (0, 1):

        @pl.loop(1, 16)
        def _(j):
            for c in stat_copies(m, j):
                c.wait_send()

    factor = scale[1]

    def text_dot(ya, yb):
        a = jnp.concatenate([cplt[pl.ds(pl.multiple_of(k * 128, 128), 128), :] for k in (ya, yb)], axis=0)
        return factor * jnp.dot(a, rows[1], preferred_element_type=F32)

    def image_dot(first):
        parts = [mod(z + first + k, NZ) for k in range(4)]
        a = jnp.concatenate([cpl[pl.ds(pl.multiple_of(k * N, N), N), :] for k in parts], axis=0)
        return factor * jnp.dot(a, cols[1], preferred_element_type=F32)

    def text_send(k, dst, sem, to):
        send(tsend.at[pl.ds(k * N, N)], dst, sem, to)

    far = text_dot(y2, yu)
    tsend[0:128, :] = far[0:128].astype(BF16)
    text_send(0, arecv.at[0], asem.at[0], up_y)
    text_send(1, arecv.at[1], asem.at[1], down_y)
    tsend[192:256, :] = far[192:256].astype(BF16)
    text_send(3, brecv.at[1], bsem.at[1], up_y)
    tacc[128:192, :] = far[128:192]
    first = 4 * mod(core + g, 2)
    isend[...] = image_dot(4 - first).astype(BF16)
    send(isend, irecv, isem.at[0], sibling)
    close = text_dot(yd, y)
    tsend[256:320, :] = close[0:64].astype(BF16)
    text_send(4, brecv.at[2], bsem.at[2], down_y)
    tacc[320:512, :] = close[64:256]
    iown[...] = image_dot(first)
    arrived(irecv, isem.at[0])
    mine_too = jnp.logical_or(g == 1, core == 1)
    down = div(first, 4)
    toward = device(xh, g, y, mod(z + 1 + 6 * down, NZ), core)

    def image_part(k):
        return pl.ds(pl.multiple_of(k * N, N), N)

    def image_sum(k):
        summed = iown[image_part(k), :] + irecv[image_part(k), :].astype(F32)
        iown[image_part(k), :] = summed
        zsend[image_part(k), :] = summed.astype(BF16)

    def image_send(k, when=None):
        to = device(xh, 0, y, mod(z + first + k, NZ), g)
        send(zsend.at[image_part(k)], zrecv.at[z], zsem.at[z], to, when)

    image_sum(3 - 2 * down)
    send(zsend.at[image_part(3 - 2 * down)], crecv, tosem.at[0], toward)
    image_sum(0)
    image_send(0, mine_too)
    image_sum(1 + 2 * down)
    image_send(1 + 2 * down)
    iown[image_part(2), :] = iown[image_part(2), :] + irecv[image_part(2), :].astype(F32)
    arrived(arecv.at[0], asem.at[0])
    tsend[128:192, :] = (tacc[128:192, :] + arecv[0].astype(F32)).astype(BF16)
    text_send(2, brecv.at[0], bsem.at[0], up_y)
    arrived(arecv.at[1], asem.at[1])
    tsend[320:384, :] = (tacc[320:384, :] + arecv[1].astype(F32)).astype(BF16)
    text_send(5, brecv.at[3], bsem.at[3], down_y)
    arrived(crecv, tosem.at[0])
    zsend[image_part(2), :] = (iown[image_part(2), :] + crecv[...].astype(F32)).astype(BF16)
    image_send(2)
    for k in (1, 2, 0, 3):
        arrived(brecv.at[k], bsem.at[k])
    for k in (0, 1):
        part = slice(384 + k * N, 384 + (k + 1) * N)
        total = tacc[part, :] + (brecv[k].astype(F32) + brecv[2 + k].astype(F32))
        tacc[part, :] = total
        xsend[k * N : (k + 1) * N, :] = total.astype(BF16)
        send(xsend.at[pl.ds(k * N, N)], xrecv.at[x], xsem.at[x], device(k, 1, y, z, core), x != 2 * k + 1)

    def received(k):
        arrived(zrecv.at[k], zsem.at[k])
        return zrecv[k].astype(F32)

    @pl.when(g == 0)
    def _():
        acc = received(mod(z + 1, NZ))
        for j in (7, 4, 2, 6):
            acc = acc + received(mod(z + j, NZ))
        tacc[0:N, :] = acc

    @pl.when(jnp.logical_and(g == 0, core == 0))
    def _():
        out[0] = tacc[0:N, :] + iown[0:N, :]

    @pl.when(jnp.logical_and(g == 0, core == 1))
    def _():
        out[0] = tacc[0:N, :] + received(z)

    @pl.when(g == 1)
    def _():
        acc = tacc[pl.ds(pl.multiple_of(384 + xh * N, N), N), :]
        for j in range(1, NX):
            k = mod(x + j, NX)
            arrived(xrecv.at[k], xsem.at[k])
            acc = acc + xrecv[k].astype(F32)
        out[0] = acc

    finish()


def per_device(teacher_image, teacher_text, student_image, student_text, scales):
    shard, width = teacher_image.shape
    assert shard == N
    dma = pltpu.SemaphoreType.DMA
    vmem = pltpu.VMEM
    teacher_image, teacher_text, student_image, student_text, scales = [
        pltpu.with_memory_space_constraint(a, pltpu.HBM)
        for a in (teacher_image, teacher_text, student_image, student_text, scales)
    ]
    any_ = pl.BlockSpec(memory_space=pltpu.HBM)
    return pl.pallas_call(
        kernel,
        out_shape=jax.ShapeDtypeStruct((1, N, width), F32),
        in_specs=[any_] * 5,
        out_specs=pl.BlockSpec(memory_space=pltpu.VMEM),
        scratch_shapes=[
            vmem((2, ROWS, width), BF16),
            vmem((2, COLS, width), BF16),
            vmem((2, ROWS, COLS), F32),
            vmem((8, 128), F32),
            vmem((2, NZ * NC, 8, 128), F32),
            vmem((2, NX * NY, 8, 128), F32),
            vmem((2, ROWS, 128), F32),
            vmem((ROWS, COLS), BF16),
            vmem((COLS, ROWS), BF16),
            vmem((COLS, width), F32),
            vmem((384, width), BF16),
            vmem((2, N, width), BF16),
            vmem((4, N, width), BF16),
            vmem((128, width), BF16),
            vmem((NX, N, width), BF16),
            vmem((256, width), BF16),
            vmem((256, width), F32),
            vmem((256, width), BF16),
            vmem((256, width), BF16),
            vmem((NZ, N, width), BF16),
            vmem((N, width), BF16),
            pltpu.SMEM((2,), F32),
            dma((5,)),
            dma((SENDS,)),
            dma((2, 2, 16)),
            dma((2, NZ)),
            dma((2, 2 * NY)),
            dma((2, NZ * NC)),
            dma((2, NX * NY)),
            dma((2,)),
            dma((4,)),
            dma((NX,)),
            dma((1,)),
            dma((NZ,)),
            dma((1,)),
        ],
        compiler_params=pltpu.CompilerParams(
            collective_id=0, has_side_effects=True, vmem_limit_bytes=48 * 2**20
        ),
    )(teacher_image, teacher_text, student_image, student_text, scales)


def solution(mesh):
    assert mesh.shape["group"] == 2 and mesh.shape["batch"] == 2 * NY * NZ * NC
    return jax.shard_map(
        per_device,
        mesh=mesh,
        in_specs=(P("batch", None), P("batch", None), P("batch", None), P("batch", None), P()),
        out_specs=P("group", "batch", None),
        check_vma=False,
    )
```

```python
import functools

import jax
import jax.numpy as jnp
from jax import lax
from jax.experimental import pallas as pl
from jax.experimental.pallas import tpu as pltpu
from jax.sharding import PartitionSpec as P

MESH = pl.DeviceIdType.MESH
F32 = jnp.float32
BF16 = jnp.bfloat16
NX, NY, NZ, NC = 4, 4, 8, 2
N = 64
ROWS = NZ * N
COLS = NY * 2 * N
SENDS = 80
FAR_FIRST = (8, 9, 7, 6, 10, 5, 11, 4, 12, 3, 13, 2, 14, 1, 15)
FAR_FIRST_PLANE = (10, 9, 11, 6, 14, 2, 8, 5, 7, 13, 15, 1, 3, 4, 12)
assert sorted(FAR_FIRST_PLANE) == sorted(FAR_FIRST)


def mod(a, n):
    return lax.rem(a, jnp.int32(n))


def div(a, n):
    return lax.div(a, jnp.int32(n))


def device(x_hi, x_lo, y, z, core):
    return {"group": x_lo, "batch": ((x_hi * NZ + z) * NY + y) * NC + core}


def kernel(
    ti, tt, si, st, scales, out,
    rows, cols, logits, stat, rstat, cstat, rcol, cpl, cplt,
    tacc, tsend, arecv, brecv, xsend, xrecv, isend, iown, irecv, zsend, zrecv, crecv, scale,
    lsem, ssem, stsem, rsem, csem, rssem, cssem, asem, bsem, xsem, isem, zsem, tosem,
):
    b = lax.axis_index("batch")
    g = lax.axis_index("group")
    core, y, z, xh = mod(b, NC), mod(div(b, NC), NY), mod(div(b, NC * NY), NZ), div(b, NC * NY * NZ)
    x = 2 * xh + g
    other = 1 - core
    step = 1 - 2 * core
    yu, yd, y2 = mod(y + 1, NY), mod(y + 3, NY), mod(y + 2, NY)
    source = core == g

    sibling = device(xh, g, y, z, other)
    up_y, down_y = device(xh, g, yu, z, core), device(xh, g, yd, z, core)
    across = device(1 - xh, 1 - g, y, z, core)
    beside = device(xh, 1 - g, y, z, core)

    pending = []

    def copy(src, dst, sem, to):
        k = len(pending)
        c = pltpu.make_async_remote_copy(
            src_ref=src, dst_ref=dst, send_sem=ssem.at[k], recv_sem=sem, device_id=to, device_id_type=MESH
        )
        return c

    def send(src, dst, sem, to, when=None):
        c = copy(src, dst, sem, to)
        pending.append((c, when))
        if when is None:
            c.start()
        else:
            pl.when(when)(c.start)

    def finish():
        assert len(pending) < SENDS
        for entry in pending:
            if entry is not None:
                c, when = entry
                if when is None:
                    c.wait_send()
                else:
                    pl.when(when)(c.wait_send)

    def arrived(dst, sem):
        pltpu.make_async_remote_copy(
            src_ref=dst, dst_ref=dst, send_sem=ssem.at[SENDS - 1], recv_sem=sem, device_id=sibling, device_id_type=MESH
        ).wait_recv()

    def row_at(m, k):
        return rows.at[m, pl.ds(pl.multiple_of(k * N, N), N)]

    def col_slot(yy, hi):
        return yy * 2 + hi

    def col_at(m, k):
        return cols.at[m, pl.ds(pl.multiple_of(k * N, N), N)]

    row_me, col_me = z * NC + core, x * NY + y

    def row_peer(j):
        q = mod(row_me + j, NZ * NC)
        return q, device(xh, g, y, div(q, NC), mod(q, NC))

    def col_peer(j):
        q = mod(col_me + j, NX * NY)
        qx = div(q, NY)
        return q, device(div(qx, 2), mod(qx, 2), mod(q, NY), z, core)

    barrier = pltpu.get_barrier_semaphore()

    near = [device(xh, g, y, mod(z + d, NZ), c) for d in (2, 6) for c in (0, 1)]
    near += [device(xh, g, y2, z, core)]
    near += [device(xh, g, y, mod(z + d, NZ), c) for d in (1, 7) for c in (0, 1)]
    near += [across, up_y, down_y, beside, sibling]
    for to in near:
        pl.semaphore_signal(barrier, inc=1, device_id=to, device_id_type=MESH)

    mine = col_slot(y, xh)
    locals_ = [
        pltpu.make_async_copy(tt, col_at(0, mine), lsem.at[0]),
        pltpu.make_async_copy(st, col_at(1, mine), lsem.at[1]),
        pltpu.make_async_copy(scales, scale, lsem.at[4]),
    ]
    row_locals = [
        pltpu.make_async_copy(ti, row_at(0, z), lsem.at[2]),
        pltpu.make_async_copy(si, row_at(1, z), lsem.at[3]),
    ]
    for c in locals_:
        c.start()

    @pl.when(source)
    def _():
        for c in row_locals:
            c.start()

    pl.semaphore_wait(barrier, len(near))
    def send_col(m, k, to):
        src = (tt, st)[m] if k is mine else col_at(m, k)
        send(src, col_at(m, k), csem.at[m, k], to)

    def send_row(m, k, to, when=None):
        src = (ti, si)[m] if k is z else row_at(m, k)
        send(src, row_at(m, k), rsem.at[m, k], to, when)

    def got_col(m, k):
        arrived(col_at(m, k), csem.at[m, k])

    def got_row(m, k):
        arrived(row_at(m, k), rsem.at[m, k])

    def z_from(d):
        return mod(z - step * d + NZ, NZ)

    def z_start(m, d):
        send_row(m, z, device(xh, g, y, mod(z + d, NZ), 0), source)
        send_row(m, z, device(xh, g, y, mod(z + NZ - d, NZ), 1), source)

    def z_own(m):
        z_start(m, 2)
        z_start(m, 1)
        send_row(m, z, sibling, source)

    def z_pass(m):
        k = z_from(2)
        got_row(m, k)
        send_row(m, k, device(xh, g, y, mod(z + 2 * step + NZ, NZ), core), core == m)
        send_row(m, k, device(xh, g, y, mod(z + step + NZ, NZ), core))
        send_row(m, k, sibling)

    def y_start(m):
        send_col(m, mine, device(xh, g, y2, z, core))
        send_col(m, mine, up_y)
        send_col(m, mine, down_y)

    def x_pass(m):
        k = col_slot(y, 1 - xh)
        got_col(m, k)
        send_col(m, k, up_y)
        send_col(m, k, down_y)

    def y_pass(m):
        k = col_slot(y2, xh)
        got_col(m, k)
        send_col(m, k, across)

    def z_rest(m):
        got_row(m, z_from(1))
        send_row(m, z_from(1), sibling)
        far = z_from(4)

        @pl.when(core == m)
        def _():
            got_row(m, far)

        send_row(m, far, sibling, core == m)
        got_row(m, z_from(3))
        send_row(m, z_from(3), sibling)

    def complete(m):
        for yy in (yu, yd):
            got_col(m, col_slot(yy, xh))
            got_col(m, col_slot(yy, 1 - xh))
        got_col(m, col_slot(y2, 1 - xh))
        for d in (1, 2, 3):
            got_row(m, mod(z + step * d + NZ, NZ))

        @pl.when(core != m)
        def _():
            got_row(m, mod(z + 4, NZ))

        @pl.when(jnp.logical_not(source))
        def _():
            got_row(m, z)

    send_col(0, mine, across)
    z_start(0, 2)
    y_start(0)
    z_start(0, 1)
    send_row(0, z, sibling, source)
    send_col(1, mine, across)
    y_start(1)
    z_start(1, 2)
    z_start(1, 1)
    send_row(1, z, sibling, source)
    x_pass(0)
    z_pass(0)
    y_pass(0)
    x_pass(1)
    z_pass(1)
    y_pass(1)
    z_rest(0)
    complete(0)
    for c in locals_:
        c.wait()

    @pl.when(source)
    def _():
        for c in row_locals:
            c.wait()

    def tile(m):
        factor = scale[m]

        logits[m] = factor * lax.dot_general(
            rows[m], cols[m], (((1,), (1,)), ((), ())), preferred_element_type=F32
        )

    def local_stats(m):
        peak, total = jnp.full((8, COLS), -3.0e38, F32), jnp.zeros((8, COLS), F32)
        row_lse = []
        for i in range(ROWS // 128):
            l = logits[m, 128 * i : 128 * (i + 1), :]
            parts = [l[:, 128 * k : 128 * (k + 1)] for k in range(COLS // 128)]
            lane_peak = functools.reduce(jnp.maximum, parts)
            lane_total = functools.reduce(jnp.add, [jnp.exp(p - lane_peak) for p in parts])
            lane_peak, lane_total = lane_peak.T, lane_total.T
            row_peak = jnp.max(lane_peak, axis=0, keepdims=True)
            row_total = jnp.sum(lane_total * jnp.exp(lane_peak - row_peak), axis=0, keepdims=True)
            row_lse.append(row_peak + jnp.log(row_total))
            l = l.reshape(16, 8, COLS)
            now = jnp.maximum(peak, jnp.max(l, axis=0))
            total = total * jnp.exp(peak - now) + jnp.sum(jnp.exp(l - now[None]), axis=0)
            peak = now
        col_peak = jnp.max(peak, axis=0, keepdims=True)
        col_lse = col_peak + jnp.log(jnp.sum(total * jnp.exp(peak - col_peak), axis=0, keepdims=True))
        parts = [col_lse[:, 128 * i : 128 * (i + 1)] for i in range(COLS // 128)]
        rest = [jnp.zeros((4, 128), F32)]
        cstat[m, col_me] = jnp.concatenate(parts + rest, axis=0)
        rstat[m, row_me] = jnp.concatenate(row_lse + rest, axis=0)

    def stat_copies(m, row_j, col_j):
        return [
            pltpu.make_async_remote_copy(
                src_ref=ref.at[m, me], dst_ref=ref.at[m, me], send_sem=stsem.at[m, kind, j], recv_sem=sem.at[m, me],
                device_id=peer(j)[1], device_id_type=MESH,
            )
            for kind, (ref, sem, me, peer, j) in enumerate(
                ((rstat, rssem, row_me, row_peer, row_j), (cstat, cssem, col_me, col_peer, col_j))
            )
        ]

    def stats_start(m):
        for row_j, col_j in zip(FAR_FIRST, FAR_FIRST_PLANE):
            for c in stat_copies(m, row_j, col_j):
                c.start()

    def joined(all_):
        peak = jnp.max(all_, axis=0)
        return peak + jnp.log(jnp.sum(jnp.exp(all_ - peak[None]), axis=0))

    def stats_end(m):
        @pl.loop(1, 16)
        def _(j):
            arrived(rstat.at[m, row_peer(j)[0]], rssem.at[m, row_peer(j)[0]])
            arrived(cstat.at[m, col_peer(j)[0]], cssem.at[m, col_peer(j)[0]])

        stat[...] = joined(cstat[m])
        turned = jnp.concatenate([joined(rstat[m]), jnp.zeros((120, 128), F32)], axis=0).T
        for i in range(ROWS // 128):
            rcol[m, 128 * i : 128 * (i + 1), :] = jnp.broadcast_to(turned[:, i : i + 1], (128, 128))
        return jnp.concatenate([stat[i : i + 1, :] for i in range(COLS // 128)], axis=1)

    def chances(m, block, col_lse):
        l = logits[m, block, :]
        r = jnp.concatenate([rcol[m, block, :]] * (COLS // 128), axis=1)
        return jnp.exp(l - r) + jnp.exp(l - col_lse)

    tile(0)
    z_rest(1)
    local_stats(0)
    stats_start(0)
    complete(1)
    tile(1)
    local_stats(1)
    stats_start(1)
    teacher_lse = stats_end(0)

    @pl.loop(0, ROWS // 128)
    def _(i):
        block = pl.ds(pl.multiple_of(i * 128, 128), 128)
        logits[0, block, :] = chances(0, block, teacher_lse)

    student_lse = stats_end(1)

    @pl.loop(0, ROWS // 128)
    def _(i):
        block = pl.ds(pl.multiple_of(i * 128, 128), 128)
        c = 0.5 * (chances(1, block, student_lse) - logits[0, block, :])
        cpl[block, :] = c.astype(BF16)
        cplt[:, block] = c.T.astype(BF16)

    for m in (0, 1):

        @pl.loop(1, 16)
        def _(j):
            for c in stat_copies(m, j, j):
                c.wait_send()

    factor = scale[1]

    def text_dot(ya, yb):
        a = jnp.concatenate([cplt[pl.ds(pl.multiple_of(k * 128, 128), 128), :] for k in (ya, yb)], axis=0)
        return factor * jnp.dot(a, rows[1], preferred_element_type=F32)

    def image_dot(first):
        parts = [mod(z + first + k, NZ) for k in range(4)]
        a = jnp.concatenate([cpl[pl.ds(pl.multiple_of(k * N, N), N), :] for k in parts], axis=0)
        return factor * jnp.dot(a, cols[1], preferred_element_type=F32)

    def text_send(k, dst, sem, to):
        send(tsend.at[pl.ds(k * N, N)], dst, sem, to)

    far = text_dot(y2, yu)
    tsend[0:128, :] = far[0:128].astype(BF16)
    text_send(0, arecv.at[0], asem.at[0], up_y)
    text_send(1, arecv.at[1], asem.at[1], down_y)
    tsend[192:256, :] = far[192:256].astype(BF16)
    text_send(3, brecv.at[1], bsem.at[1], up_y)
    tacc[128:192, :] = far[128:192]
    first = 4 * mod(core + g, 2)
    isend[...] = image_dot(4 - first).astype(BF16)
    send(isend, irecv, isem.at[0], sibling)
    close = text_dot(yd, y)
    tsend[256:320, :] = close[0:64].astype(BF16)
    text_send(4, brecv.at[2], bsem.at[2], down_y)
    tacc[320:512, :] = close[64:256]
    iown[...] = image_dot(first)
    arrived(irecv, isem.at[0])
    mine_too = jnp.logical_or(g == 1, core == 1)
    down = div(first, 4)
    toward = device(xh, g, y, mod(z + 1 + 6 * down, NZ), core)

    def image_part(k):
        return pl.ds(pl.multiple_of(k * N, N), N)

    def image_sum(k):
        summed = iown[image_part(k), :] + irecv[image_part(k), :].astype(F32)
        iown[image_part(k), :] = summed
        zsend[image_part(k), :] = summed.astype(BF16)

    def image_send(k, when=None):
        to = device(xh, 0, y, mod(z + first + k, NZ), g)
        send(zsend.at[image_part(k)], zrecv.at[z], zsem.at[z], to, when)

    image_sum(3 - 2 * down)
    send(zsend.at[image_part(3 - 2 * down)], crecv, tosem.at[0], toward)
    image_sum(0)
    image_send(0, mine_too)
    image_sum(1 + 2 * down)
    image_send(1 + 2 * down)
    iown[image_part(2), :] = iown[image_part(2), :] + irecv[image_part(2), :].astype(F32)
    arrived(arecv.at[0], asem.at[0])
    tsend[128:192, :] = (tacc[128:192, :] + arecv[0].astype(F32)).astype(BF16)
    text_send(2, brecv.at[0], bsem.at[0], up_y)
    arrived(arecv.at[1], asem.at[1])
    tsend[320:384, :] = (tacc[320:384, :] + arecv[1].astype(F32)).astype(BF16)
    text_send(5, brecv.at[3], bsem.at[3], down_y)
    arrived(crecv, tosem.at[0])
    zsend[image_part(2), :] = (iown[image_part(2), :] + crecv[...].astype(F32)).astype(BF16)
    image_send(2)
    for k in (1, 2, 0, 3):
        arrived(brecv.at[k], bsem.at[k])
    for k in (0, 1):
        part = slice(384 + k * N, 384 + (k + 1) * N)
        total = tacc[part, :] + (brecv[k].astype(F32) + brecv[2 + k].astype(F32))
        tacc[part, :] = total
        xsend[k * N : (k + 1) * N, :] = total.astype(BF16)
        send(xsend.at[pl.ds(k * N, N)], xrecv.at[x], xsem.at[x], device(k, 1, y, z, core), x != 2 * k + 1)

    def received(k):
        arrived(zrecv.at[k], zsem.at[k])
        return zrecv[k].astype(F32)

    @pl.when(g == 0)
    def _():
        acc = received(mod(z + 1, NZ))
        for j in (7, 4, 2, 6):
            acc = acc + received(mod(z + j, NZ))
        tacc[0:N, :] = acc

    @pl.when(jnp.logical_and(g == 0, core == 0))
    def _():
        out[0] = tacc[0:N, :] + iown[0:N, :]

    @pl.when(jnp.logical_and(g == 0, core == 1))
    def _():
        out[0] = tacc[0:N, :] + received(z)

    @pl.when(g == 1)
    def _():
        acc = tacc[pl.ds(pl.multiple_of(384 + xh * N, N), N), :]
        for j in range(1, NX):
            k = mod(x + j, NX)
            arrived(xrecv.at[k], xsem.at[k])
            acc = acc + xrecv[k].astype(F32)
        out[0] = acc

    finish()


def per_device(teacher_image, teacher_text, student_image, student_text, scales):
    shard, width = teacher_image.shape
    assert shard == N
    dma = pltpu.SemaphoreType.DMA
    vmem = pltpu.VMEM
    teacher_image, teacher_text, student_image, student_text, scales = [
        pltpu.with_memory_space_constraint(a, pltpu.HBM)
        for a in (teacher_image, teacher_text, student_image, student_text, scales)
    ]
    any_ = pl.BlockSpec(memory_space=pltpu.HBM)
    return pl.pallas_call(
        kernel,
        out_shape=jax.ShapeDtypeStruct((1, N, width), F32),
        in_specs=[any_] * 5,
        out_specs=pl.BlockSpec(memory_space=pltpu.VMEM),
        scratch_shapes=[
            vmem((2, ROWS, width), BF16),
            vmem((2, COLS, width), BF16),
            vmem((2, ROWS, COLS), F32),
            vmem((8, 128), F32),
            vmem((2, NZ * NC, 8, 128), F32),
            vmem((2, NX * NY, 8, 128), F32),
            vmem((2, ROWS, 128), F32),
            vmem((ROWS, COLS), BF16),
            vmem((COLS, ROWS), BF16),
            vmem((COLS, width), F32),
            vmem((384, width), BF16),
            vmem((2, N, width), BF16),
            vmem((4, N, width), BF16),
            vmem((128, width), BF16),
            vmem((NX, N, width), BF16),
            vmem((256, width), BF16),
            vmem((256, width), F32),
            vmem((256, width), BF16),
            vmem((256, width), BF16),
            vmem((NZ, N, width), BF16),
            vmem((N, width), BF16),
            pltpu.SMEM((2,), F32),
            dma((5,)),
            dma((SENDS,)),
            dma((2, 2, 16)),
            dma((2, NZ)),
            dma((2, 2 * NY)),
            dma((2, NZ * NC)),
            dma((2, NX * NY)),
            dma((2,)),
            dma((4,)),
            dma((NX,)),
            dma((1,)),
            dma((NZ,)),
            dma((1,)),
        ],
        compiler_params=pltpu.CompilerParams(
            collective_id=0, has_side_effects=True, vmem_limit_bytes=48 * 2**20
        ),
    )(teacher_image, teacher_text, student_image, student_text, scales)


def solution(mesh):
    assert mesh.shape["group"] == 2 and mesh.shape["batch"] == 2 * NY * NZ * NC
    return jax.shard_map(
        per_device,
        mesh=mesh,
        in_specs=(P("batch", None), P("batch", None), P("batch", None), P("batch", None), P()),
        out_specs=P("group", "batch", None),
        check_vma=False,
    )
```
